256 devices in a mesh: member: 64 (over z_lo, x, y, core), shard: 4 (over z_hi).
Axes of the slice: x: 4, y: 4, z: 8 (z_hi: 4, z_lo: 2; z = z_hi * 2 + z_lo), core: 2. Of those that a mesh axis runs over, the one named last changes fastest.
Arguments:
- processor_latent: bfloat16 [64, 128, 1024], P('member', 'shard'), may hold values from -240 to 240
- stencil_index: int32 [4, 3, 768], P('shard'), may hold values from 0 to 127
- interp_weight: float32 [4, 3, 768], P('shard'), may hold values from 0.1 to 1
- prev_state: float32 [4, 112, 768], P('shard'), may hold values from -6 to 6
- observed: float32 [4, 112, 768], P('shard', None, 'member'), may hold values from -6 to 6
- cell_area: float32 [4, 768], P('shard', 'member'), may hold values from 0.5 to 2
- var_weight: float32 [112], replicated, may hold values from 1 to 16
- hidden_weight: bfloat16 [1024, 1024], replicated, may hold values from -0.1875 to 0.1875
- hidden_bias: float32 [1024], replicated, may hold values from -3 to 3
- output_weight: bfloat16 [1024, 112], replicated, may hold values from -0.1875 to 0.1875
- output_bias: float32 [112], replicated, may hold values from -3 to 3
Outputs:
- mesh_grad: float32 [64, 128, 1024], P('member', 'shard')
The draws below stay inside these ranges and needn't reach their ends.
Inputs may be any that keep to these rules, and one draw needn't show every extreme that they name: `stencil_index`: rows of the same member's mesh.
All inputs are finite; a program needn't handle non-finite values.
Results may differ from the reference program's by a relative error of at most 0.019.
Values may be sent and summed in bfloat16 or wider, within the bound.
A program may use at most 64 MiB of HBM per device.

```python
import math
import jax
import jax.numpy as jnp
from jax import lax

H = 1024
VARS = 112
K = 3
CELL_DEV = 768
MEMBER_COUNT = 64
SLABS = 4
MESH = 128


def draw_processor_latent(key, part):
    base_key = jax.random.fold_in(jax.random.fold_in(key, 17), 0)
    column_key = jax.random.fold_in(jax.random.fold_in(key, 17), 1)
    row_key = jax.random.fold_in(jax.random.fold_in(key, 17), 2)
    wobble_key = jax.random.fold_in(jax.random.fold_in(key, 17), 4)
    spread_key = jax.random.fold_in(jax.random.fold_in(key, 17), 5)
    columns = jnp.exp(jax.random.uniform(column_key, (1, 1, H), jnp.float32) * math.log(10.0))
    row_scale = jnp.exp(jax.random.uniform(row_key, (1, MESH, 1), jnp.float32) * math.log(4.0))
    shared = jnp.clip(jax.random.normal(base_key, (1, MESH, H), jnp.float32), -5.0, 5.0)
    member_spread = jnp.exp(math.log(0.01) + jax.random.uniform(spread_key, (MEMBER_COUNT, MESH, 1), jnp.float32) * math.log(4.0))
    wobble = jnp.clip(jax.random.normal(wobble_key, (MEMBER_COUNT, MESH, H), jnp.float32), -3.0, 3.0)
    return (shared * columns * row_scale * (1.0 + member_spread * wobble)).astype(jnp.bfloat16)


def with_ends(drawn, own_key, low, top_value):
    longest = drawn.shape.index(max(drawn.shape))
    spots = []
    for shift in (0, 1):
        where = [jax.random.randint(jax.random.fold_in(own_key, axis), (), 0, length) for axis, length in enumerate(drawn.shape)]
        where[longest] = (where[longest] + shift) % drawn.shape[longest]
        spots.append(tuple(where))
    return drawn.at[spots[0]].set(low).at[spots[1]].set(top_value)


def level_of(key, extent, cuts, low, high):
    level, own = 1.0, jax.random.fold_in(key, 6)
    for position, blocks in cuts:
        heights = jnp.exp(jax.random.uniform(jax.random.fold_in(own, position), (blocks,), jnp.float32, low / len(cuts), high / len(cuts)))
        level = level * jnp.repeat(heights, extent[position] // blocks).reshape([-1 if axis == position else 1 for axis in range(len(extent))])
    return level


def normal_values(key, dims, scale, most, cuts=(), held_as=jnp.bfloat16):
    array = scale * jax.random.normal(key, dims, jnp.float32)
    if cuts:
        array = array * level_of(key, dims, cuts, -0.22, 0.18)
    return jnp.clip(array, -most, most).astype(held_as)


def setup_inputs(seed: int = 0) -> dict:
    keys = jax.random.split(jax.random.key(seed), 12)
    processor_latent = draw_processor_latent(jax.random.fold_in(keys[11], 71), 0)
    stencil_index = with_ends(jax.random.randint(keys[1], (SLABS, K, CELL_DEV), 0, MESH), jax.random.fold_in(keys[1], 1), 0, MESH - 1).astype(jnp.int32)
    interp_weight = jnp.clip(0.1 + 0.9 * jax.random.uniform(keys[2], (SLABS, K, CELL_DEV), jnp.float32) ** level_of(keys[2], (SLABS, K, CELL_DEV), ((0, 4),), -0.2, 0.2), 0.1, 1.0)
    prev_state = normal_values(keys[3], (SLABS, VARS, CELL_DEV), 1.0, 6.0, ((0, 4),), jnp.float32)
    observed = normal_values(keys[4], (SLABS, VARS, CELL_DEV), 1.0, 6.0, ((0, 4), (2, 64)), jnp.float32)
    cell_area = jnp.clip(jnp.exp(math.log(2.0) - 1.3862944 * jax.random.uniform(keys[5], (SLABS, CELL_DEV), jnp.float32) ** level_of(keys[5], (SLABS, CELL_DEV), ((0, 4), (1, 64)), -0.2, 0.2)), 0.5, 2.0)
    var_weight = jnp.clip(jnp.exp(jax.random.uniform(keys[6], (VARS,), jnp.float32, math.log(1.0), math.log(16.0))), 1.0, 16.0)
    hidden_weight = normal_values(keys[7], (H, H), H ** -0.5, 0.1875)
    hidden_bias = normal_values(keys[8], (H,), 0.5, 3.0, (), jnp.float32)
    output_weight = normal_values(keys[9], (H, VARS), H ** -0.5, 0.1875)
    output_bias = normal_values(keys[10], (VARS,), 0.5, 3.0, (), jnp.float32)
    return {"processor_latent": processor_latent, "stencil_index": stencil_index, "interp_weight": interp_weight, "prev_state": prev_state, "observed": observed, "cell_area": cell_area, "var_weight": var_weight, "hidden_weight": hidden_weight, "hidden_bias": hidden_bias, "output_weight": output_weight, "output_bias": output_bias}


smoothing = 0.05
fairness = 0.95
epsilon = 1e-05

def softened_slope(differ):
    return differ / jnp.sqrt(differ * differ + smoothing * smoothing)

def normalize(latent):
    average = lax.optimization_barrier(jnp.mean(latent, axis=1, keepdims=True))
    centred = latent - average
    inverse = lax.rsqrt(lax.optimization_barrier(jnp.mean(centred * centred, axis=1, keepdims=True)) + epsilon)
    return (centred * inverse, inverse)

def interpolate(mesh_rows, stencil, weights):
    picked = jnp.take(mesh_rows, stencil, axis=0).astype(jnp.float32)
    return lax.optimization_barrier(jnp.sum(picked * weights[:, :, None], axis=0))

def flatten_cells(stacked):
    return jnp.transpose(stacked, (1, 0, 2)).reshape(stacked.shape[1], -1)

def reference(processor_latent, stencil_index, interp_weight, prev_state, observed, cell_area, var_weight, hidden_weight, hidden_bias, output_weight, output_bias):
    stencil = flatten_cells(stencil_index).astype(jnp.int32)
    weights = flatten_cells(interp_weight)
    previous = flatten_cells(prev_state)
    observed_truth = flatten_cells(observed)
    area_row = cell_area.reshape(-1)

    def forward_crps(mesh_rows):
        normal_form, inverse = normalize(interpolate(mesh_rows, stencil, weights))
        normed = normal_form.astype(jnp.bfloat16)
        pre_act = jnp.dot(normed, hidden_weight, preferred_element_type=jnp.float32) + hidden_bias
        hidden = jax.nn.silu(pre_act).astype(jnp.bfloat16)
        update = lax.dot_general(output_weight, hidden, (((0,), (1,)), ((), ())), preferred_element_type=jnp.float32)
        return (previous + (update + output_bias[:, None]), pre_act)
    member_prediction, hidden_preactivation = lax.map(forward_crps, processor_latent)
    fairness_factor = (1.0 - fairness) / MEMBER_COUNT

    def pairwise_total(member_slice):
        return lax.optimization_barrier(jnp.sum(softened_slope(member_slice[None] - member_prediction), axis=0))
    pairwise_sums = lax.map(pairwise_total, member_prediction)
    loss_weighting = area_row[None, None, :] * var_weight[None, :, None]
    upstream_gradient = (loss_weighting * (softened_slope(member_prediction - observed_truth[None]) - (1.0 - fairness_factor) / (MEMBER_COUNT - 1) * pairwise_sums)).astype(jnp.bfloat16)

    def backward(packed):
        mesh_rows, pre_act, cotangent_m = packed
        normal_form, inverse = normalize(interpolate(mesh_rows, stencil, weights))
        grad_hidden = lax.dot_general(cotangent_m, output_weight, (((0,), (1,)), ((), ())), preferred_element_type=jnp.float32)
        logistic = jax.nn.sigmoid(pre_act)
        grad_pre = (grad_hidden * (logistic * (1.0 + pre_act * (1.0 - logistic)))).astype(jnp.bfloat16)
        grad_normed = lax.dot_general(grad_pre, hidden_weight, (((1,), (1,)), ((), ())), preferred_element_type=jnp.float32)
        grad_cell = inverse * (grad_normed - lax.optimization_barrier(jnp.mean(grad_normed, axis=1, keepdims=True)) - normal_form * lax.optimization_barrier(jnp.mean(grad_normed * normal_form, axis=1, keepdims=True)))
        spread = (weights[:, :, None] * grad_cell[None]).reshape(-1, grad_cell.shape[1])
        return jax.ops.segment_sum(spread, stencil.reshape(-1), num_segments=MESH)
    return lax.map(backward, (processor_latent, hidden_preactivation, upstream_gradient))
```

```python
import jax
import jax.numpy as jnp
from jax import lax
from jax.experimental import pallas as pl
from jax.experimental.pallas import tpu as pltpu
from jax.sharding import PartitionSpec as P

smoothing = 0.05
fairness = 0.95
epsilon = 1e-05

MESH_ID = pl.DeviceIdType.MESH
F32 = jnp.float32
BF16 = jnp.bfloat16
NN = (((1,), (0,)), ((), ()))
NT = (((1,), (1,)), ((), ()))


def slope(differ):
    return differ * lax.rsqrt(differ * differ + smoothing * smoothing)


def dot(a, b, dims, precision=None):
    return lax.dot_general(a, b, dims, precision=precision, preferred_element_type=F32)


def split(value):
    high = value.astype(BF16)
    return high, (value - high.astype(F32)).astype(BF16)


def kernel(
    members,
    mesh_in,
    stencil_in,
    weight_in,
    prev_in,
    observed_in,
    area_in,
    var_in,
    hidden_in,
    hidden_bias_in,
    output_in,
    output_bias_in,
    out_ref,
    gathered,
    stencil,
    weight,
    prev,
    observed,
    area,
    var,
    hidden,
    hidden_bias,
    output,
    output_bias,
    cells_mat,
    mesh_split,
    blend,
    blend_t,
    product,
    slope_act,
    grad_side,
    target,
    coefficient,
    forecast_out,
    forecast_in,
    state,
    sums,
    cot_out,
    cot_in,
    part_out,
    part_hop,
    part_in,
    local_sem,
    gather_send,
    gather_recv,
    cast_send,
    cast_recv,
    back_send,
    back_recv,
    part_send,
    part_recv,
):
    me = lax.axis_index("member")
    spot = lax.axis_index("shard")
    right = lax.rem(spot + 1, 4)
    left = lax.rem(spot + 3, 4)
    across = lax.rem(spot + 2, 4)
    variables = 112
    chunk_rows = 192

    loads = [
        pltpu.make_async_copy(source, target_ref, local_sem.at[number])
        for number, (source, target_ref) in enumerate(
            (
                (mesh_in, gathered.at[pl.ds(2 * spot, 2)]),
                (stencil_in, stencil),
                (weight_in, weight),
                (prev_in, prev),
                (observed_in, observed),
                (area_in, area),
                (var_in, var),
                (hidden_in, hidden),
                (hidden_bias_in, hidden_bias),
                (output_in, output.at[pl.ds(0, variables)]),
                (output_bias_in, output_bias),
            )
        )
    ]
    for load in loads:
        load.start()

    barrier = pltpu.get_barrier_semaphore()

    @pl.loop(1, members)
    def _(offset):
        pl.semaphore_signal(
            barrier,
            inc=1,
            device_id={"member": lax.rem(me + offset, members)},
            device_id_type=MESH_ID,
        )

    for neighbour in (left, right):
        pl.semaphore_signal(
            barrier, inc=1, device_id={"shard": neighbour}, device_id_type=MESH_ID
        )
    pl.semaphore_wait(barrier, members + 1)

    def gather_copy(number, source, slot, to):
        return pltpu.make_async_remote_copy(
            src_ref=source,
            dst_ref=gathered.at[slot],
            send_sem=gather_send.at[number],
            recv_sem=gather_recv.at[number],
            device_id={"shard": to},
            device_id_type=MESH_ID,
        )

    own = [
        gather_copy(0, mesh_in.at[0], 2 * spot, right),
        gather_copy(1, mesh_in.at[1], 2 * spot + 1, left),
        gather_copy(2, mesh_in.at[1], 2 * spot + 1, right),
        gather_copy(3, mesh_in.at[0], 2 * spot, left),
    ]
    for copy in own:
        copy.start()

    for load in loads[1:7]:
        load.wait()
    loads[10].wait()
    row_ids = lax.broadcasted_iota(jnp.int32, (128, 768), 0)
    cells_t = jnp.zeros((128, 768), F32)
    for k in range(3):
        cells_t = cells_t + jnp.where(stencil[k] == row_ids, weight[k], 0.0)
    cells_mat[...] = cells_t.T

    own[0].wait_recv()
    relay_right = gather_copy(4, gathered.at[2 * left], 2 * left, right)
    relay_right.start()
    own[1].wait_recv()
    relay_left = gather_copy(5, gathered.at[2 * right + 1], 2 * right + 1, left)
    relay_left.start()

    slots = lax.broadcasted_iota(jnp.int32, (16, 768), 0)
    slots = jnp.where(slots < 12, slots, slots - 4)
    chosen = jnp.where(
        lax.broadcasted_iota(jnp.int32, (16, 768), 1) == slots + 12 * me, 1.0, 0.0
    ).astype(F32)
    target[...] = jnp.zeros((16, 128), F32)
    for slot in range(16):
        cell = slot if slot < 12 else slot - 4
        target[slot : slot + 1, :variables] = observed[cell] - output_bias[...]
    target[:, :variables] = target[:, :variables] - dot(
        chosen, prev[...], NT, lax.Precision.HIGHEST
    )
    lanes = lax.broadcasted_iota(jnp.int32, (16, 12), 1)
    cell_ids = lax.broadcasted_iota(jnp.int32, (16, 12), 0)
    cell_ids = jnp.where(cell_ids < 12, cell_ids, cell_ids - 4)
    area_column = jnp.sum(
        jnp.where(lanes == cell_ids, area[...], 0.0), axis=1, keepdims=True
    )
    coefficient[...] = jnp.zeros((16, 128), F32)
    coefficient[:, :variables] = area_column * var[...]
    output[variables:, :] = jnp.zeros((128 - variables, 1024), BF16)

    own[2].wait_recv()
    own[3].wait_recv()
    relay_right.wait_recv()
    relay_left.wait_recv()
    loads[0].wait()
    loads[7].wait()
    loads[8].wait()
    loads[9].wait()

    rows = gathered[...].reshape(128, 1024).astype(F32)
    rows = rows - jnp.mean(rows, axis=1, keepdims=True)
    row_high, row_low = split(rows)
    mesh_split[:128] = row_high
    mesh_split[128:] = row_low
    gram_parts = dot(mesh_split[...], mesh_split[:128], NT)
    gram = (gram_parts[:128] + gram_parts[128:] + gram_parts[128:].T) * (1.0 / 1024)
    through_parts = dot(mesh_split[...], hidden[...], NN)
    through = through_parts[:128] + through_parts[128:]
    through_high, through_low = split(through)
    through_all = jnp.concatenate([through_high, through_low, through_high], axis=0)
    cells = cells_mat[...]
    variance = jnp.sum(
        cells * dot(cells, gram, NN, lax.Precision.HIGHEST), axis=1, keepdims=True
    )
    scaled = cells * lax.rsqrt(variance + epsilon)
    cells_mat[...] = scaled
    scaled_high, scaled_low = split(scaled)
    blend[:, :128] = scaled_high
    blend[:, 128:256] = scaled_high
    blend[:, 256:] = scaled_low

    def cast_copy(to):
        return pltpu.make_async_remote_copy(
            src_ref=forecast_out.at[to],
            dst_ref=forecast_in.at[me],
            send_sem=cast_send,
            recv_sem=cast_recv,
            device_id={"member": to},
            device_id_type=MESH_ID,
        )

    @pl.loop(0, 4)
    def _(step):
        part = lax.rem(lax.div(me, 16) + step, 4)
        span = pl.ds(pl.multiple_of(part * chunk_rows, chunk_rows), chunk_rows)
        raw = dot(blend[span], through_all, NN)
        product[span] = raw
        act = raw + hidden_bias[...]
        active = act * (0.5 * jnp.tanh(0.5 * act) + 0.5)
        update = dot(active.astype(BF16), output[...], NT)
        for piece in range(48):
            forecast_out[part * 16 + piece // 3, piece % 3] = update[
                piece * 4 : piece * 4 + 4
            ]

        @pl.loop(0, 16)
        def _(offset):
            to = part * 16 + lax.rem(me + 1 + offset, 16)

            @pl.when(to != me)
            def _():
                cast_copy(to).start()

    forecast_in[me] = forecast_out[me]
    blend_t[...] = cells_mat[...].T.astype(BF16)

    @pl.loop(0, 4)
    def _(part):
        span = pl.ds(pl.multiple_of(part * chunk_rows, chunk_rows), chunk_rows)
        act = product[span] + hidden_bias[...]
        gate = 0.5 * jnp.tanh(0.5 * act) + 0.5
        slope_act[span] = gate * (1.0 + act * (1.0 - gate))

    others = pl.ds(0, members - 1)
    pltpu.make_async_copy(forecast_in.at[others], forecast_in.at[others], cast_recv).wait()

    for m in range(64):
        state[m] = jnp.concatenate([forecast_in[m, 0], forecast_in[m, 1]], axis=0)
    for m in range(32):
        state[64 + m] = jnp.concatenate([forecast_in[m, 2], forecast_in[m + 32, 2]], axis=0)

    def half_turn(value):
        return pltpu.roll(value, 4, 0)

    @pl.loop(0, 8)
    def _(block):
        base = block * 8
        values = [state[base + i] for i in range(8)]
        totals = [jnp.zeros((8, 128), F32) for _ in range(8)]
        for i in range(8):
            for j in range(i + 1, 8):
                push = slope(values[i] - values[j])
                totals[i] = totals[i] + push
                totals[j] = totals[j] - push
        for i in range(8):
            sums[base + i] = totals[i]

    @pl.loop(0, 28)
    def _(step):
        first = lax.rem(step, 8) * 8
        second = lax.rem(lax.rem(step, 8) + lax.div(step, 8) + 1, 8) * 8
        values = [state[first + i] for i in range(8)]
        totals = [sums[first + i] for i in range(8)]
        for j in range(8):
            other = state[second + j]
            total = sums[second + j]
            for i in range(8):
                push = slope(values[i] - other)
                totals[i] = totals[i] + push
                total = total - push
            sums[second + j] = total
        for i in range(8):
            sums[first + i] = totals[i]

    @pl.loop(0, 4)
    def _(block):
        base = 64 + block * 8
        values = [state[base + i] for i in range(8)]
        turned = [half_turn(value) for value in values]
        totals = [slope(values[i] - turned[i]) for i in range(8)]
        crossed = [jnp.zeros((8, 128), F32) for _ in range(8)]
        for i in range(8):
            for j in range(i + 1, 8):
                push = slope(values[i] - values[j])
                totals[i] = totals[i] + push
                totals[j] = totals[j] - push
                push = slope(values[i] - turned[j])
                totals[i] = totals[i] + push
                crossed[j] = crossed[j] - push
        for i in range(8):
            sums[base + i] = totals[i] + half_turn(crossed[i])

    @pl.loop(0, 6)
    def _(step):
        first = 64 + lax.rem(step, 4) * 8
        second = 64 + lax.rem(lax.rem(step, 4) + lax.div(step, 4) + 1, 4) * 8
        values = [state[first + i] for i in range(8)]
        totals = [sums[first + i] for i in range(8)]
        for j in range(8):
            other = state[second + j]
            turned = half_turn(other)
            total = sums[second + j]
            crossed = jnp.zeros((8, 128), F32)
            for i in range(8):
                push = slope(values[i] - other)
                totals[i] = totals[i] + push
                total = total - push
                push = slope(values[i] - turned)
                totals[i] = totals[i] + push
                crossed = crossed - push
            sums[second + j] = total + half_turn(crossed)
        for i in range(8):
            sums[first + i] = totals[i]

    pair_factor = (1.0 - (1.0 - fairness) / members) / (members - 1)

    def back_copy(to):
        return pltpu.make_async_remote_copy(
            src_ref=cot_out.at[to],
            dst_ref=cot_in.at[me],
            send_sem=back_send,
            recv_sem=back_recv,
            device_id={"member": to},
            device_id_type=MESH_ID,
        )

    @pl.loop(0, 32)
    def _(m):
        for extra in (0, 32):
            cot = coefficient[:8] * (
                slope(state[m + extra] - target[:8]) - pair_factor * sums[m + extra]
            )
            cot_out[m + extra, 0] = cot[:4].astype(BF16)
            cot_out[m + extra, 1] = cot[4:].astype(BF16)
        cot = coefficient[8:] * (
            slope(state[64 + m] - target[8:]) - pair_factor * sums[64 + m]
        )
        cot_out[m, 2] = cot[:4].astype(BF16)
        cot_out[m + 32, 2] = cot[4:].astype(BF16)

    @pl.loop(1, members)
    def _(offset):
        back_copy(lax.rem(me + offset, members)).start()

    cot_in[me] = cot_out[me]
    pltpu.make_async_copy(cot_in.at[others], cot_in.at[others], back_recv).wait()

    @pl.loop(0, 4)
    def _(part):
        span = pl.ds(pl.multiple_of(part * chunk_rows, chunk_rows), chunk_rows)
        cot = jnp.concatenate(
            [cot_in[part * 16 + piece // 3, piece % 3].astype(F32) for piece in range(48)],
            axis=0,
        ).astype(BF16)
        grad = dot(cot, output[...], NN) * slope_act[span]
        grad_side[span, :1024] = grad.astype(BF16)
        along = jnp.sum(grad * product[span], axis=1, keepdims=True) * (1.0 / 1024)
        grad_side[span, 1024:] = (cells_mat[span] * along).astype(BF16)

    joined = dot(blend_t[...], grad_side[...], NN)
    result = dot(joined[:, :1024].astype(BF16), hidden[...], NT)
    result = result - dot(joined[:, 1024:].astype(BF16), mesh_split[:128], NN)
    result = result - jnp.mean(result, axis=1, keepdims=True)
    product[:128] = result
    part_out[...] = result.astype(BF16).reshape(8, 16, 1024)

    def part_copy(number, source, slot, to):
        return pltpu.make_async_remote_copy(
            src_ref=source,
            dst_ref=part_in.at[slot],
            send_sem=part_send.at[number],
            recv_sem=part_recv.at[number],
            device_id={"shard": to},
            device_id_type=MESH_ID,
        )

    hops = [
        part_copy(0, part_out.at[2 * across], 0, right),
        part_copy(1, part_out.at[2 * across + 1], 1, left),
        part_copy(2, part_out.at[2 * right + 1], 2, right),
        part_copy(3, part_out.at[2 * left], 3, left),
    ]
    for hop in hops:
        hop.start()
    def tile(slot):
        return product[pl.ds(pl.multiple_of(slot * 16, 16), 16)]

    hops[0].wait_recv()
    part_hop[0] = (part_in[0].astype(F32) + tile(2 * right)).astype(BF16)
    hops.append(part_copy(4, part_hop.at[0], 4, right))
    hops[4].start()
    hops[1].wait_recv()
    part_hop[1] = (part_in[1].astype(F32) + tile(2 * left + 1)).astype(BF16)
    hops.append(part_copy(5, part_hop.at[1], 5, left))
    hops[5].start()
    for hop in hops[2:]:
        hop.wait_recv()
    out_ref[:16] = tile(2 * spot) + part_in[4].astype(F32) + part_in[3].astype(F32)
    out_ref[16:] = tile(2 * spot + 1) + part_in[2].astype(F32) + part_in[5].astype(F32)

    for copy in own + [relay_right, relay_left] + hops:
        copy.wait_send()
    pltpu.make_async_copy(forecast_out.at[others], forecast_out.at[others], cast_send).wait()
    pltpu.make_async_copy(cot_out.at[others], cot_out.at[others], back_send).wait()


def local(
    processor_latent,
    stencil_index,
    interp_weight,
    prev_state,
    observed,
    cell_area,
    var_weight,
    hidden_weight,
    hidden_bias,
    output_weight,
    output_bias,
):
    members = lax.axis_size("member")
    operands = (
        processor_latent.reshape(2, 16, 1024),
        jnp.transpose(stencil_index, (1, 0, 2)),
        jnp.transpose(interp_weight, (1, 0, 2)),
        prev_state[0],
        jnp.transpose(observed, (2, 0, 1)),
        cell_area,
        var_weight.reshape(1, -1),
        hidden_weight,
        hidden_bias.reshape(1, -1),
        output_weight.T,
        output_bias.reshape(1, -1),
    )

    def body(*refs):
        kernel(members, *refs)

    vmem = pltpu.VMEM
    dma = pltpu.SemaphoreType.DMA
    out = pl.pallas_call(
        body,
        name="decoder_step",
        out_shape=jax.ShapeDtypeStruct((32, 1024), F32),
        in_specs=[pl.BlockSpec(memory_space=pl.ANY)] * len(operands),
        out_specs=pl.BlockSpec(memory_space=pltpu.VMEM),
        scratch_shapes=[
            vmem((8, 16, 1024), BF16),
            vmem((3, 1, 768), jnp.int32),
            vmem((3, 1, 768), F32),
            vmem((112, 768), F32),
            vmem((12, 1, 112), F32),
            vmem((1, 12), F32),
            vmem((1, 112), F32),
            vmem((1024, 1024), BF16),
            vmem((1, 1024), F32),
            vmem((128, 1024), BF16),
            vmem((1, 112), F32),
            vmem((768, 128), F32),
            vmem((256, 1024), BF16),
            vmem((768, 384), BF16),
            vmem((128, 768), BF16),
            vmem((768, 1024), F32),
            vmem((768, 1024), F32),
            vmem((768, 1152), BF16),
            vmem((16, 128), F32),
            vmem((16, 128), F32),
            vmem((64, 3, 4, 128), F32),
            vmem((64, 3, 4, 128), F32),
            vmem((96, 8, 128), F32),
            vmem((96, 8, 128), F32),
            vmem((64, 3, 4, 128), BF16),
            vmem((64, 3, 4, 128), BF16),
            vmem((8, 16, 1024), BF16),
            vmem((2, 16, 1024), BF16),
            vmem((6, 16, 1024), BF16),
            dma((11,)),
            dma((6,)),
            dma((6,)),
            dma,
            dma,
            dma,
            dma,
            dma((6,)),
            dma((6,)),
        ],
        compiler_params=pltpu.CompilerParams(collective_id=0, has_side_effects=True),
    )(*operands)
    return out[None]


def solution(mesh):
    in_specs = (
        P("member", "shard", None),
        P("shard", None, None),
        P("shard", None, None),
        P("shard", None, None),
        P("shard", None, "member"),
        P("shard", "member"),
        P(),
        P(),
        P(),
        P(),
        P(),
    )
    out_specs = P("member", "shard", None)
    return jax.shard_map(local, mesh=mesh, in_specs=in_specs, out_specs=out_specs, check_vma=False)
```

```python
import jax
import jax.numpy as jnp
from jax import lax
from jax.experimental import pallas as pl
from jax.experimental.pallas import tpu as pltpu
from jax.sharding import PartitionSpec as P

smoothing = 0.05
fairness = 0.95
epsilon = 1e-05

MESH_ID = pl.DeviceIdType.MESH
F32 = jnp.float32
BF16 = jnp.bfloat16
NN = (((1,), (0,)), ((), ()))
NT = (((1,), (1,)), ((), ()))
VARS = 112


def slope(differ):
    return differ * lax.rsqrt(differ * differ + smoothing * smoothing)


def dot(a, b, dims, precision=None):
    return lax.dot_general(a, b, dims, precision=precision, preferred_element_type=F32)


def split(value):
    high = value.astype(BF16)
    return high, (value - high.astype(F32)).astype(BF16)


def ring():
    spot = lax.axis_index("shard")
    return spot, lax.rem(spot + 1, 4), lax.rem(spot + 3, 4), lax.rem(spot + 2, 4)


def signal(barrier, axis, to):
    pl.semaphore_signal(barrier, inc=1, device_id={axis: to}, device_id_type=MESH_ID)


def gather_kernel(
    mesh_in,
    stencil_in,
    weight_in,
    prev_in,
    observed_in,
    area_in,
    var_in,
    output_bias_in,
    hidden_in,
    hidden_bias_in,
    output_in,
    gathered,
    cells_ref,
    target,
    coefficient,
    hidden,
    hidden_bias,
    output,
    stencil,
    weight,
    prev,
    observed,
    area,
    var,
    output_bias,
    local_sem,
    send_sem,
    recv_sem,
):
    me = lax.axis_index("member")
    spot, right, left, _ = ring()
    barrier = pltpu.get_barrier_semaphore()
    for neighbour in (left, right):
        signal(barrier, "shard", neighbour)
    loads = [
        pltpu.make_async_copy(source, place, local_sem.at[number])
        for number, (source, place) in enumerate(
            (
                (stencil_in, stencil),
                (weight_in, weight),
                (prev_in, prev),
                (observed_in, observed),
                (area_in, area),
                (var_in, var),
                (output_bias_in, output_bias),
                (mesh_in, gathered.at[pl.ds(2 * spot, 2)]),
                (hidden_in, hidden),
                (hidden_bias_in, hidden_bias),
                (output_in, output.at[pl.ds(0, VARS)]),
            )
        )
    ]
    for load in loads:
        load.start()
    pl.semaphore_wait(barrier, 2)

    def copy(number, source, slot, to):
        return pltpu.make_async_remote_copy(
            src_ref=source,
            dst_ref=gathered.at[slot],
            send_sem=send_sem.at[number],
            recv_sem=recv_sem.at[number],
            device_id={"shard": to},
            device_id_type=MESH_ID,
        )

    own = [
        copy(0, mesh_in.at[0], 2 * spot, right),
        copy(1, mesh_in.at[1], 2 * spot + 1, left),
        copy(2, mesh_in.at[1], 2 * spot + 1, right),
        copy(3, mesh_in.at[0], 2 * spot, left),
    ]
    for each in own:
        each.start()
    for load in loads[:7]:
        load.wait()

    row_ids = lax.broadcasted_iota(jnp.int32, (128, 768), 0)
    cells_t = jnp.zeros((128, 768), F32)
    for k in range(3):
        cells_t = cells_t + jnp.where(stencil[k] == row_ids, weight[k], 0.0)
    natural = lax.broadcasted_iota(jnp.int32, (768, 768), 1)
    place = lax.broadcasted_iota(jnp.int32, (768, 768), 0)
    cell_of = jnp.where(
        place < 512,
        lax.shift_right_logical(place, 3) * 12 + (place & 7),
        lax.shift_right_logical(place - 512, 2) * 12 + 8 + (place & 3),
    )
    order = jnp.where(natural == cell_of, 1.0, 0.0).astype(BF16)
    high, rest = split(cells_t)
    middle = (cells_t - high.astype(F32)) - rest.astype(F32)
    cells_ref[...] = (
        dot(order, high, NT) + dot(order, rest, NT) + dot(order, middle.astype(BF16), NT)
    )

    slots = lax.broadcasted_iota(jnp.int32, (16, 768), 0)
    slots = jnp.where(slots < 12, slots, slots - 4)
    chosen = jnp.where(
        lax.broadcasted_iota(jnp.int32, (16, 768), 1) == slots + 12 * me, 1.0, 0.0
    ).astype(F32)
    target[...] = jnp.zeros((16, 128), F32)
    for slot in range(16):
        cell = slot if slot < 12 else slot - 4
        target[slot : slot + 1, :VARS] = observed[cell] - output_bias[...]
    target[:, :VARS] = target[:, :VARS] - dot(chosen, prev[...], NT, lax.Precision.HIGHEST)
    lanes = lax.broadcasted_iota(jnp.int32, (16, 12), 1)
    cell_ids = lax.broadcasted_iota(jnp.int32, (16, 12), 0)
    cell_ids = jnp.where(cell_ids < 12, cell_ids, cell_ids - 4)
    area_column = jnp.sum(
        jnp.where(lanes == cell_ids, area[...], 0.0), axis=1, keepdims=True
    )
    coefficient[...] = jnp.zeros((16, 128), F32)
    coefficient[:, :VARS] = area_column * var[...]

    own[0].wait_recv()
    relay_right = copy(4, gathered.at[2 * left], 2 * left, right)
    relay_right.start()
    own[1].wait_recv()
    relay_left = copy(5, gathered.at[2 * right + 1], 2 * right + 1, left)
    relay_left.start()
    output[VARS:] = jnp.zeros((128 - VARS, 1024), BF16)
    for load in loads[7:]:
        load.wait()
    for each in own[2:] + [relay_right, relay_left]:
        each.wait_recv()
    for each in own + [relay_right, relay_left]:
        each.wait_send()


def score_kernel(
    members,
    gathered,
    cells_ref,
    target,
    coefficient,
    hidden,
    hidden_bias,
    output,
    out_ref,
    blend,
    blend_t,
    product,
    slope_act,
    grad_side,
    joined,
    forecast_out_a,
    forecast_out_b,
    forecast_in_a,
    forecast_in_b,
    state_b,
    sums_a,
    sums_b,
    cot_out_a,
    cot_out_b,
    cot_in_a,
    cot_in_b,
    result_ref,
    part_out,
    part_hop,
    part_in,
    cast_send,
    cast_recv,
    back_send,
    back_recv,
    part_send,
    part_recv,
):
    me = lax.axis_index("member")
    spot, right, left, across = ring()
    barrier = pltpu.get_barrier_semaphore()

    @pl.loop(1, members)
    def _(offset):
        signal(barrier, "member", lax.rem(me + offset, members))

    for neighbour in (left, right):
        signal(barrier, "shard", neighbour)

    rows_low = gathered[...].reshape(128, 1024)
    rows = rows_low.astype(F32)
    average = jnp.mean(rows, axis=1, keepdims=True)
    row_high, row_low = split(rows - average)
    cross = dot(row_low, row_high, NT)
    gram = (dot(row_high, row_high, NT) + cross + cross.T) * (1.0 / 1024)
    through_all = dot(
        jnp.concatenate([rows_low, jnp.ones((16, 1024), BF16)], axis=0), hidden[...], NN
    )
    through = through_all[:128] - average * through_all[128:129]
    through_high, through_low = split(through)
    stack = jnp.concatenate([through_high, through_low, through_high], axis=0)
    cells = cells_ref[...]
    variance = jnp.sum(
        cells * dot(cells, gram, NN, lax.Precision.HIGHEST), axis=1, keepdims=True
    )
    scaled = cells * lax.rsqrt(variance + epsilon)
    scaled_high, scaled_low = split(scaled)
    blend[:, :128] = scaled_high
    blend[:, 128:256] = scaled_high
    blend[:, 256:] = scaled_low

    def exchange(source, place, to, send, recv):
        return pltpu.make_async_remote_copy(
            src_ref=source.at[to],
            dst_ref=place.at[me],
            send_sem=send,
            recv_sem=recv,
            device_id={"member": to},
            device_id_type=MESH_ID,
        )

    def send_forecast(source, place, number, first, count):
        @pl.loop(0, count)
        def _(offset):
            to = first + lax.rem(me + 1 + offset, count)

            @pl.when(to != me)
            def _():
                exchange(source, place, to, cast_send.at[number], cast_recv.at[number]).start()

    def updates(span):
        raw = dot(blend[span], stack, NN)
        product[span] = raw
        act = raw + hidden_bias[...]
        active = act * (0.5 * jnp.tanh(0.5 * act) + 0.5)
        return dot(active.astype(BF16), output[...], NT)

    pl.semaphore_wait(barrier, members + 1)

    @pl.loop(0, 4)
    def _(step):
        part = lax.rem(lax.div(me, 16) + 1 + step, 4)
        update = updates(pl.ds(pl.multiple_of(part * 128, 128), 128))
        forecast_out_a[pl.ds(part * 16, 16)] = update.reshape(16, 8, 128)
        send_forecast(forecast_out_a, forecast_in_a, 0, part * 16, 16)

    @pl.loop(0, 2)
    def _(step):
        part = lax.rem(lax.div(me, 32) + 1 + step, 2)
        update = updates(pl.ds(pl.multiple_of(512 + part * 128, 128), 128))
        for piece in range(32):
            forecast_out_b[part * 32 + piece] = update[piece * 4 : piece * 4 + 4]
        send_forecast(forecast_out_b, forecast_in_b, 1, part * 32, 32)

    forecast_in_a[me] = forecast_out_a[me]
    forecast_in_b[me] = forecast_out_b[me]
    blend_t[...] = blend[:, :128].astype(F32).T.astype(BF16)

    @pl.loop(0, 6)
    def _(part):
        span = pl.ds(pl.multiple_of(part * 128, 128), 128)
        act = product[span] + hidden_bias[...]
        gate = 0.5 * jnp.tanh(0.5 * act) + 0.5
        slope_act[span] = gate * (1.0 + act * (1.0 - gate))

    others = pl.ds(0, members - 1)

    def settle(ref, sem):
        pltpu.make_async_copy(ref.at[others], ref.at[others], sem).wait()

    settle(forecast_in_a, cast_recv.at[0])

    @pl.loop(0, 8)
    def _(block):
        base = block * 8
        values = [forecast_in_a[base + i] for i in range(8)]
        totals = [jnp.zeros((8, 128), F32) for _ in range(8)]
        for i in range(8):
            for j in range(i + 1, 8):
                push = slope(values[i] - values[j])
                totals[i] = totals[i] + push
                totals[j] = totals[j] - push
        for i in range(8):
            sums_a[base + i] = totals[i]

    @pl.loop(0, 28)
    def _(step):
        first = lax.rem(step, 8) * 8
        second = lax.rem(lax.rem(step, 8) + lax.div(step, 8) + 1, 8) * 8
        values = [forecast_in_a[first + i] for i in range(8)]
        totals = [sums_a[first + i] for i in range(8)]
        for j in range(8):
            other = forecast_in_a[second + j]
            total = sums_a[second + j]
            for i in range(8):
                push = slope(values[i] - other)
                totals[i] = totals[i] + push
                total = total - push
            sums_a[second + j] = total
        for i in range(8):
            sums_a[first + i] = totals[i]

    pair_factor = (1.0 - (1.0 - fairness) / members) / (members - 1)

    @pl.loop(0, 8)
    def _(block):
        for i in range(8):
            m = block * 8 + i
            cot_out_a[m] = (
                coefficient[:8]
                * (slope(forecast_in_a[m] - target[:8]) - pair_factor * sums_a[m])
            ).astype(BF16)

    def send_back(source, place, number):
        @pl.loop(1, members)
        def _(offset):
            to = lax.rem(me + offset, members)
            exchange(source, place, to, back_send.at[number], back_recv.at[number]).start()

    send_back(cot_out_a, cot_in_a, 0)
    cot_in_a[me] = cot_out_a[me]

    settle(forecast_in_b, cast_recv.at[1])
    for m in range(32):
        state_b[m] = jnp.concatenate([forecast_in_b[m], forecast_in_b[m + 32]], axis=0)

    def half_turn(value):
        return pltpu.roll(value, 4, 0)

    @pl.loop(0, 4)
    def _(block):
        base = block * 8
        values = [state_b[base + i] for i in range(8)]
        turned = [half_turn(value) for value in values]
        totals = [slope(values[i] - turned[i]) for i in range(8)]
        crossed = [jnp.zeros((8, 128), F32) for _ in range(8)]
        for i in range(8):
            for j in range(i + 1, 8):
                push = slope(values[i] - values[j])
                totals[i] = totals[i] + push
                totals[j] = totals[j] - push
                push = slope(values[i] - turned[j])
                totals[i] = totals[i] + push
                crossed[j] = crossed[j] - push
        for i in range(8):
            sums_b[base + i] = totals[i] + half_turn(crossed[i])

    @pl.loop(0, 6)
    def _(step):
        first = lax.rem(step, 4) * 8
        second = lax.rem(lax.rem(step, 4) + lax.div(step, 4) + 1, 4) * 8
        values = [state_b[first + i] for i in range(8)]
        totals = [sums_b[first + i] for i in range(8)]
        for j in range(8):
            other = state_b[second + j]
            turned = half_turn(other)
            total = sums_b[second + j]
            crossed = jnp.zeros((8, 128), F32)
            for i in range(8):
                push = slope(values[i] - other)
                totals[i] = totals[i] + push
                total = total - push
                push = slope(values[i] - turned)
                totals[i] = totals[i] + push
                crossed = crossed - push
            sums_b[second + j] = total + half_turn(crossed)
        for i in range(8):
            sums_b[first + i] = totals[i]

    @pl.loop(0, 8)
    def _(block):
        for i in range(4):
            m = block * 4 + i
            cot = coefficient[8:] * (
                slope(state_b[m] - target[8:]) - pair_factor * sums_b[m]
            )
            cot_out_b[m] = cot[:4].astype(BF16)
            cot_out_b[m + 32] = cot[4:].astype(BF16)

    send_back(cot_out_b, cot_in_b, 1)
    cot_in_b[me] = cot_out_b[me]

    def backward(cot, span):
        grad = dot(cot, output[...], NN) * slope_act[span]
        grad_side[span, :1024] = grad.astype(BF16)
        along = jnp.sum(grad * product[span], axis=1, keepdims=True) * (1.0 / 1024)
        grad_side[span, 1024:] = (blend[span, :128].astype(F32) * along).astype(BF16)

    settle(cot_in_a, back_recv.at[0])

    @pl.loop(0, 4)
    def _(part):
        cot = cot_in_a[pl.ds(part * 16, 16)].astype(F32).reshape(128, 128).astype(BF16)
        backward(cot, pl.ds(pl.multiple_of(part * 128, 128), 128))

    joined[...] = dot(blend_t[:, :512], grad_side[:512], NN)
    settle(cot_in_b, back_recv.at[1])

    @pl.loop(0, 2)
    def _(part):
        cot = jnp.concatenate(
            [cot_in_b[part * 32 + piece].astype(F32) for piece in range(32)], axis=0
        ).astype(BF16)
        backward(cot, pl.ds(pl.multiple_of(512 + part * 128, 128), 128))

    total = joined[...] + dot(blend_t[:, 512:], grad_side[512:], NN)
    outer = total[:, :1024].astype(BF16)
    inner = total[:, 1024:].astype(BF16)
    result = dot(outer, hidden[...], NT)
    result = result - dot(inner, gathered[...].reshape(128, 1024), NN)
    result = result - jnp.mean(result, axis=1, keepdims=True)
    result_ref[...] = result.reshape(8, 16, 1024)
    part_out[...] = result.astype(BF16).reshape(8, 16, 1024)

    def part_copy(number, source, to):
        return pltpu.make_async_remote_copy(
            src_ref=source,
            dst_ref=part_in.at[number],
            send_sem=part_send.at[number],
            recv_sem=part_recv.at[number],
            device_id={"shard": to},
            device_id_type=MESH_ID,
        )

    hops = [
        part_copy(0, part_out.at[2 * across], right),
        part_copy(1, part_out.at[2 * across + 1], left),
        part_copy(2, part_out.at[2 * right + 1], right),
        part_copy(3, part_out.at[2 * left], left),
        part_copy(4, part_hop.at[0], right),
        part_copy(5, part_hop.at[1], left),
    ]
    for hop in hops[:4]:
        hop.start()
    hops[0].wait_recv()
    part_hop[0] = (part_in[0].astype(F32) + result_ref[2 * right]).astype(BF16)
    hops[4].start()
    hops[1].wait_recv()
    part_hop[1] = (part_in[1].astype(F32) + result_ref[2 * left + 1]).astype(BF16)
    hops[5].start()
    for hop in hops[2:]:
        hop.wait_recv()
    out_ref[:16] = result_ref[2 * spot] + part_in[4].astype(F32) + part_in[3].astype(F32)
    out_ref[16:] = result_ref[2 * spot + 1] + part_in[2].astype(F32) + part_in[5].astype(F32)

    for hop in hops:
        hop.wait_send()
    settle(forecast_out_a, cast_send.at[0])
    settle(forecast_out_b, cast_send.at[1])
    settle(cot_out_a, back_send.at[0])
    settle(cot_out_b, back_send.at[1])


def local(
    processor_latent,
    stencil_index,
    interp_weight,
    prev_state,
    observed,
    cell_area,
    var_weight,
    hidden_weight,
    hidden_bias,
    output_weight,
    output_bias,
):
    members = lax.axis_size("member")
    vmem = pltpu.VMEM
    dma = pltpu.SemaphoreType.DMA
    outside = pl.BlockSpec(memory_space=pltpu.MemorySpace.HBM)
    inside = pl.BlockSpec(memory_space=pltpu.VMEM)
    staged = pl.pallas_call(
        gather_kernel,
        name="gather_rows",
        out_shape=(
            jax.ShapeDtypeStruct((8, 16, 1024), BF16),
            jax.ShapeDtypeStruct((768, 128), F32),
            jax.ShapeDtypeStruct((16, 128), F32),
            jax.ShapeDtypeStruct((16, 128), F32),
            jax.ShapeDtypeStruct((1024, 1024), BF16),
            jax.ShapeDtypeStruct((1, 1024), F32),
            jax.ShapeDtypeStruct((128, 1024), BF16),
        ),
        in_specs=[outside] * 11,
        out_specs=(inside,) * 7,
        scratch_shapes=[
            vmem((3, 1, 768), jnp.int32),
            vmem((3, 1, 768), F32),
            vmem((112, 768), F32),
            vmem((12, 1, 112), F32),
            vmem((1, 12), F32),
            vmem((1, 112), F32),
            vmem((1, 112), F32),
            dma((11,)),
            dma((6,)),
            dma((6,)),
        ],
        compiler_params=pltpu.CompilerParams(
            collective_id=0, has_side_effects=True, vmem_limit_bytes=16 << 20
        ),
    )(
        *(
            pltpu.with_memory_space_constraint(each, pltpu.MemorySpace.HBM)
            for each in (
                processor_latent.reshape(2, 16, 1024),
                jnp.transpose(stencil_index, (1, 0, 2)),
                jnp.transpose(interp_weight, (1, 0, 2)),
                prev_state[0],
                jnp.transpose(observed, (2, 0, 1)),
                cell_area,
                var_weight.reshape(1, -1),
                output_bias.reshape(1, -1),
                hidden_weight,
                hidden_bias.reshape(1, -1),
                output_weight.T,
            )
        )
    )

    def body(*refs):
        score_kernel(members, *refs)

    out = pl.pallas_call(
        body,
        name="score_step",
        out_shape=jax.ShapeDtypeStruct((32, 1024), F32),
        in_specs=[inside] * 7,
        out_specs=inside,
        scratch_shapes=[
            vmem((768, 384), BF16),
            vmem((128, 768), BF16),
            vmem((768, 1024), F32),
            vmem((768, 1024), F32),
            vmem((768, 1152), BF16),
            vmem((128, 1152), F32),
            vmem((64, 8, 128), F32),
            vmem((64, 4, 128), F32),
            vmem((64, 8, 128), F32),
            vmem((64, 4, 128), F32),
            vmem((32, 8, 128), F32),
            vmem((64, 8, 128), F32),
            vmem((32, 8, 128), F32),
            vmem((64, 8, 128), BF16),
            vmem((64, 4, 128), BF16),
            vmem((64, 8, 128), BF16),
            vmem((64, 4, 128), BF16),
            vmem((8, 16, 1024), F32),
            vmem((8, 16, 1024), BF16),
            vmem((2, 16, 1024), BF16),
            vmem((6, 16, 1024), BF16),
            dma((2,)),
            dma((2,)),
            dma((2,)),
            dma((2,)),
            dma((6,)),
            dma((6,)),
        ],
        compiler_params=pltpu.CompilerParams(
            collective_id=1, has_side_effects=True, vmem_limit_bytes=28 << 20
        ),
    )(*staged)
    return out[None]


def solution(mesh):
    in_specs = (
        P("member", "shard", None),
        P("shard", None, None),
        P("shard", None, None),
        P("shard", None, None),
        P("shard", None, "member"),
        P("shard", "member"),
        P(),
        P(),
        P(),
        P(),
        P(),
    )
    out_specs = P("member", "shard", None)
    return jax.shard_map(local, mesh=mesh, in_specs=in_specs, out_specs=out_specs, check_vma=False)
```

```python
import jax
import jax.numpy as jnp
from jax import lax
from jax.experimental import pallas as pl
from jax.experimental.pallas import tpu as pltpu
from jax.sharding import PartitionSpec as P

smoothing = 0.05
fairness = 0.95
epsilon = 1e-05

MESH_ID = pl.DeviceIdType.MESH
F32 = jnp.float32
BF16 = jnp.bfloat16
NN = (((1,), (0,)), ((), ()))
NT = (((1,), (1,)), ((), ()))
VARS = 112


def slope(differ):
    return differ * lax.rsqrt(differ * differ + smoothing * smoothing)


def dot(a, b, dims, precision=None):
    return lax.dot_general(a, b, dims, precision=precision, preferred_element_type=F32)


def split(value):
    high = value.astype(BF16)
    return high, (value - high.astype(F32)).astype(BF16)


def ring():
    spot = lax.axis_index("shard")
    return spot, lax.rem(spot + 1, 4), lax.rem(spot + 3, 4), lax.rem(spot + 2, 4)


def signal(barrier, axis, to):
    pl.semaphore_signal(barrier, inc=1, device_id={axis: to}, device_id_type=MESH_ID)


def member_lines(me):
    core = lax.rem(me, 2)
    y = lax.rem(lax.div(me, 2), 4)
    x = lax.rem(lax.div(me, 8), 4)
    z = lax.div(me, 32)
    x_line = [me + 8 * (lax.rem(x + step, 4) - x) for step in (1, 2, 3)]
    y_line = [me + 2 * (lax.rem(y + step, 4) - y) for step in (1, 2, 3)]
    return x_line, y_line, [me + 32 * (1 - 2 * z)], [me + 1 - 2 * core]


def step_kernel(
    members,
    mesh_in,
    stencil_in,
    weight_in,
    prev_in,
    observed_in,
    area_in,
    var_in,
    hidden_in,
    hidden_bias_in,
    output_in,
    output_bias_in,
    out_ref,
    gathered,
    stencil,
    weight,
    prev,
    observed,
    area,
    var,
    output_bias,
    hidden,
    hidden_bias,
    output,
    cells_mat,
    target,
    coefficient,
    blend,
    blend_t,
    product,
    slope_act,
    grad_side,
    joined,
    forecast_out_a,
    forecast_out_b,
    forecast_in_a,
    forecast_in_b,
    state_b,
    sums_a,
    sums_b,
    cot_out_a,
    cot_out_b,
    cot_in_a,
    cot_in_b,
    result_ref,
    part_out,
    part_hop,
    part_in,
    local_sem,
    known,
    gather_send,
    gather_recv,
    cast_send,
    cast_recv,
    back_send,
    back_recv,
    part_send,
    part_recv,
):
    me = lax.axis_index("member")
    spot, right, left, across = ring()
    lines = member_lines(me)
    barrier = pltpu.get_barrier_semaphore()
    for neighbour in (left, right):
        signal(barrier, "shard", neighbour)
    for line in lines:
        for peer in line:
            signal(barrier, "member", peer)
    loads = [
        pltpu.make_async_copy(source, place, local_sem.at[number])
        for number, (source, place) in enumerate(
            (
                (stencil_in, stencil),
                (weight_in, weight),
                (prev_in, prev),
                (observed_in, observed),
                (area_in, area),
                (var_in, var),
                (output_bias_in, output_bias),
                (mesh_in, gathered.at[pl.ds(2 * spot, 2)]),
                (hidden_in, hidden),
                (hidden_bias_in, hidden_bias),
                (output_in, output.at[pl.ds(0, VARS)]),
            )
        )
    ]
    for load in loads:
        load.start()
    pl.semaphore_wait(barrier, 10)
    for peer in lines[0]:
        signal(known.at[0], "member", peer)

    def copy(number, source, slot, to):
        return pltpu.make_async_remote_copy(
            src_ref=source,
            dst_ref=gathered.at[slot],
            send_sem=gather_send.at[number],
            recv_sem=gather_recv.at[number],
            device_id={"shard": to},
            device_id_type=MESH_ID,
        )

    own = [
        copy(0, mesh_in.at[0], 2 * spot, right),
        copy(1, mesh_in.at[1], 2 * spot + 1, left),
        copy(2, mesh_in.at[1], 2 * spot + 1, right),
        copy(3, mesh_in.at[0], 2 * spot, left),
    ]
    for each in own:
        each.start()
    for load in loads[:7]:
        load.wait()

    row_ids = lax.broadcasted_iota(jnp.int32, (128, 768), 0)
    cells_t = jnp.zeros((128, 768), F32)
    for k in range(3):
        cells_t = cells_t + jnp.where(stencil[k] == row_ids, weight[k], 0.0)
    natural = lax.broadcasted_iota(jnp.int32, (768, 768), 1)
    place = lax.broadcasted_iota(jnp.int32, (768, 768), 0)
    cell_of = jnp.where(
        place < 512,
        lax.shift_right_logical(place, 3) * 12 + (place & 7),
        lax.shift_right_logical(place - 512, 2) * 12 + 8 + (place & 3),
    )
    order = jnp.where(natural == cell_of, 1.0, 0.0).astype(BF16)
    high, rest = split(cells_t)
    middle = (cells_t - high.astype(F32)) - rest.astype(F32)
    cells_mat[...] = (
        dot(order, high, NT) + dot(order, rest, NT) + dot(order, middle.astype(BF16), NT)
    )

    slots = lax.broadcasted_iota(jnp.int32, (16, 768), 0)
    slots = jnp.where(slots < 12, slots, slots - 4)
    chosen = jnp.where(
        lax.broadcasted_iota(jnp.int32, (16, 768), 1) == slots + 12 * me, 1.0, 0.0
    ).astype(F32)
    target[...] = jnp.zeros((16, 128), F32)
    for slot in range(16):
        cell = slot if slot < 12 else slot - 4
        target[slot : slot + 1, :VARS] = observed[cell] - output_bias[...]
    target[:, :VARS] = target[:, :VARS] - dot(chosen, prev[...], NT, lax.Precision.HIGHEST)
    lanes = lax.broadcasted_iota(jnp.int32, (16, 12), 1)
    cell_ids = lax.broadcasted_iota(jnp.int32, (16, 12), 0)
    cell_ids = jnp.where(cell_ids < 12, cell_ids, cell_ids - 4)
    area_column = jnp.sum(
        jnp.where(lanes == cell_ids, area[...], 0.0), axis=1, keepdims=True
    )
    coefficient[...] = jnp.zeros((16, 128), F32)
    coefficient[:, :VARS] = area_column * var[...]

    pl.semaphore_wait(known.at[0], 3)
    for peer in lines[1]:
        signal(known.at[1], "member", peer)
    own[0].wait_recv()
    relay_right = copy(4, gathered.at[2 * left], 2 * left, right)
    relay_right.start()
    own[1].wait_recv()
    relay_left = copy(5, gathered.at[2 * right + 1], 2 * right + 1, left)
    relay_left.start()
    pl.semaphore_wait(known.at[1], 3)
    for peer in lines[2]:
        signal(known.at[2], "member", peer)
    output[VARS:] = jnp.zeros((128 - VARS, 1024), BF16)
    for load in loads[7:]:
        load.wait()
    for each in own[2:] + [relay_right, relay_left]:
        each.wait_recv()

    rows_low = gathered[...].reshape(128, 1024)
    rows = rows_low.astype(F32)
    average = jnp.mean(rows, axis=1, keepdims=True)
    row_high, row_low = split(rows - average)
    cross = dot(row_low, row_high, NT)
    gram = (dot(row_high, row_high, NT) + cross + cross.T) * (1.0 / 1024)
    through_all = dot(
        jnp.concatenate([rows_low, jnp.ones((16, 1024), BF16)], axis=0), hidden[...], NN
    )
    through = through_all[:128] - average * through_all[128:129]
    through_high, through_low = split(through)
    stack = jnp.concatenate([through_high, through_low, through_high], axis=0)
    cells = cells_mat[...]
    variance = jnp.sum(
        cells * dot(cells, gram, NN, lax.Precision.HIGHEST), axis=1, keepdims=True
    )
    scaled = cells * lax.rsqrt(variance + epsilon)
    scaled_high, scaled_low = split(scaled)
    blend[:, :128] = scaled_high
    blend[:, 128:256] = scaled_high
    blend[:, 256:] = scaled_low

    def exchange(source, place, to, send, recv):
        return pltpu.make_async_remote_copy(
            src_ref=source.at[to],
            dst_ref=place.at[me],
            send_sem=send,
            recv_sem=recv,
            device_id={"member": to},
            device_id_type=MESH_ID,
        )

    def send_forecast(source, place, number, first, count):
        @pl.loop(0, count)
        def _(offset):
            to = first + lax.rem(me + 1 + offset, count)

            @pl.when(to != me)
            def _():
                exchange(source, place, to, cast_send.at[number], cast_recv.at[number]).start()

    def updates(span):
        raw = dot(blend[span], stack, NN)
        product[span] = raw
        act = raw + hidden_bias[...]
        active = act * (0.5 * jnp.tanh(0.5 * act) + 0.5)
        return dot(active.astype(BF16), output[...], NT)

    pl.semaphore_wait(known.at[2], 1)

    @pl.loop(0, 4)
    def _(step):
        part = lax.rem(lax.div(me, 16) + 1 + step, 4)
        update = updates(pl.ds(pl.multiple_of(part * 128, 128), 128))
        forecast_out_a[pl.ds(part * 16, 16)] = update.reshape(16, 8, 128)
        send_forecast(forecast_out_a, forecast_in_a, 0, part * 16, 16)

    @pl.loop(0, 2)
    def _(step):
        part = lax.rem(lax.div(me, 32) + 1 + step, 2)
        update = updates(pl.ds(pl.multiple_of(512 + part * 128, 128), 128))
        for piece in range(32):
            forecast_out_b[part * 32 + piece] = update[piece * 4 : piece * 4 + 4]
        send_forecast(forecast_out_b, forecast_in_b, 1, part * 32, 32)

    forecast_in_a[me] = forecast_out_a[me]
    forecast_in_b[me] = forecast_out_b[me]
    blend_t[...] = blend[:, :128].astype(F32).T.astype(BF16)

    @pl.loop(0, 6)
    def _(part):
        span = pl.ds(pl.multiple_of(part * 128, 128), 128)
        act = product[span] + hidden_bias[...]
        gate = 0.5 * jnp.tanh(0.5 * act) + 0.5
        slope_act[span] = gate * (1.0 + act * (1.0 - gate))

    others = pl.ds(0, members - 1)

    def settle(ref, sem):
        pltpu.make_async_copy(ref.at[others], ref.at[others], sem).wait()

    settle(forecast_in_a, cast_recv.at[0])

    @pl.loop(0, 8)
    def _(block):
        base = block * 8
        values = [forecast_in_a[base + i] for i in range(8)]
        totals = [jnp.zeros((8, 128), F32) for _ in range(8)]
        for i in range(8):
            for j in range(i + 1, 8):
                push = slope(values[i] - values[j])
                totals[i] = totals[i] + push
                totals[j] = totals[j] - push
        for i in range(8):
            sums_a[base + i] = totals[i]

    @pl.loop(0, 28)
    def _(step):
        first = lax.rem(step, 8) * 8
        second = lax.rem(lax.rem(step, 8) + lax.div(step, 8) + 1, 8) * 8
        values = [forecast_in_a[first + i] for i in range(8)]
        totals = [sums_a[first + i] for i in range(8)]
        for j in range(8):
            other = forecast_in_a[second + j]
            total = sums_a[second + j]
            for i in range(8):
                push = slope(values[i] - other)
                totals[i] = totals[i] + push
                total = total - push
            sums_a[second + j] = total
        for i in range(8):
            sums_a[first + i] = totals[i]

    pair_factor = (1.0 - (1.0 - fairness) / members) / (members - 1)

    @pl.loop(0, 8)
    def _(block):
        for i in range(8):
            m = block * 8 + i
            cot_out_a[m] = (
                coefficient[:8]
                * (slope(forecast_in_a[m] - target[:8]) - pair_factor * sums_a[m])
            ).astype(BF16)

    def send_back(source, place, number):
        @pl.loop(1, members)
        def _(offset):
            to = lax.rem(me + offset, members)
            exchange(source, place, to, back_send.at[number], back_recv.at[number]).start()

    send_back(cot_out_a, cot_in_a, 0)
    cot_in_a[me] = cot_out_a[me]

    settle(forecast_in_b, cast_recv.at[1])
    for m in range(32):
        state_b[m] = jnp.concatenate([forecast_in_b[m], forecast_in_b[m + 32]], axis=0)

    def half_turn(value):
        return pltpu.roll(value, 4, 0)

    @pl.loop(0, 4)
    def _(block):
        base = block * 8
        values = [state_b[base + i] for i in range(8)]
        turned = [half_turn(value) for value in values]
        totals = [slope(values[i] - turned[i]) for i in range(8)]
        crossed = [jnp.zeros((8, 128), F32) for _ in range(8)]
        for i in range(8):
            for j in range(i + 1, 8):
                push = slope(values[i] - values[j])
                totals[i] = totals[i] + push
                totals[j] = totals[j] - push
                push = slope(values[i] - turned[j])
                totals[i] = totals[i] + push
                crossed[j] = crossed[j] - push
        for i in range(8):
            sums_b[base + i] = totals[i] + half_turn(crossed[i])

    @pl.loop(0, 6)
    def _(step):
        first = lax.rem(step, 4) * 8
        second = lax.rem(lax.rem(step, 4) + lax.div(step, 4) + 1, 4) * 8
        values = [state_b[first + i] for i in range(8)]
        totals = [sums_b[first + i] for i in range(8)]
        for j in range(8):
            other = state_b[second + j]
            turned = half_turn(other)
            total = sums_b[second + j]
            crossed = jnp.zeros((8, 128), F32)
            for i in range(8):
                push = slope(values[i] - other)
                totals[i] = totals[i] + push
                total = total - push
                push = slope(values[i] - turned)
                totals[i] = totals[i] + push
                crossed = crossed - push
            sums_b[second + j] = total + half_turn(crossed)
        for i in range(8):
            sums_b[first + i] = totals[i]

    @pl.loop(0, 8)
    def _(block):
        for i in range(4):
            m = block * 4 + i
            cot = coefficient[8:] * (
                slope(state_b[m] - target[8:]) - pair_factor * sums_b[m]
            )
            cot_out_b[m] = cot[:4].astype(BF16)
            cot_out_b[m + 32] = cot[4:].astype(BF16)

    send_back(cot_out_b, cot_in_b, 1)
    cot_in_b[me] = cot_out_b[me]

    def backward(cot, span):
        grad = dot(cot, output[...], NN) * slope_act[span]
        grad_side[span, :1024] = grad.astype(BF16)
        along = jnp.sum(grad * product[span], axis=1, keepdims=True) * (1.0 / 1024)
        grad_side[span, 1024:] = (blend[span, :128].astype(F32) * along).astype(BF16)

    settle(cot_in_a, back_recv.at[0])

    @pl.loop(0, 4)
    def _(part):
        cot = cot_in_a[pl.ds(part * 16, 16)].astype(F32).reshape(128, 128).astype(BF16)
        backward(cot, pl.ds(pl.multiple_of(part * 128, 128), 128))

    joined[...] = dot(blend_t[:, :512], grad_side[:512], NN)
    settle(cot_in_b, back_recv.at[1])

    @pl.loop(0, 2)
    def _(part):
        cot = jnp.concatenate(
            [cot_in_b[part * 32 + piece].astype(F32) for piece in range(32)], axis=0
        ).astype(BF16)
        backward(cot, pl.ds(pl.multiple_of(512 + part * 128, 128), 128))

    total = joined[...] + dot(blend_t[:, 512:], grad_side[512:], NN)
    outer = total[:, :1024].astype(BF16)
    inner = total[:, 1024:].astype(BF16)
    result = dot(outer, hidden[...], NT)
    result = result - dot(inner, gathered[...].reshape(128, 1024), NN)
    result = result - jnp.mean(result, axis=1, keepdims=True)
    result_ref[...] = result.reshape(8, 16, 1024)
    part_out[...] = result.astype(BF16).reshape(8, 16, 1024)

    def part_copy(number, source, to):
        return pltpu.make_async_remote_copy(
            src_ref=source,
            dst_ref=part_in.at[number],
            send_sem=part_send.at[number],
            recv_sem=part_recv.at[number],
            device_id={"shard": to},
            device_id_type=MESH_ID,
        )

    hops = [
        part_copy(0, part_out.at[2 * across], right),
        part_copy(1, part_out.at[2 * across + 1], left),
        part_copy(2, part_out.at[2 * right + 1], right),
        part_copy(3, part_out.at[2 * left], left),
        part_copy(4, part_hop.at[0], right),
        part_copy(5, part_hop.at[1], left),
    ]
    for hop in hops[:4]:
        hop.start()
    hops[0].wait_recv()
    part_hop[0] = (part_in[0].astype(F32) + result_ref[2 * right]).astype(BF16)
    hops[4].start()
    hops[1].wait_recv()
    part_hop[1] = (part_in[1].astype(F32) + result_ref[2 * left + 1]).astype(BF16)
    hops[5].start()
    for hop in hops[2:]:
        hop.wait_recv()
    out_ref[:16] = result_ref[2 * spot] + part_in[4].astype(F32) + part_in[3].astype(F32)
    out_ref[16:] = result_ref[2 * spot + 1] + part_in[2].astype(F32) + part_in[5].astype(F32)

    for each in own + [relay_right, relay_left] + hops:
        each.wait_send()
    settle(forecast_out_a, cast_send.at[0])
    settle(forecast_out_b, cast_send.at[1])
    settle(cot_out_a, back_send.at[0])
    settle(cot_out_b, back_send.at[1])


def local(
    processor_latent,
    stencil_index,
    interp_weight,
    prev_state,
    observed,
    cell_area,
    var_weight,
    hidden_weight,
    hidden_bias,
    output_weight,
    output_bias,
):
    members = lax.axis_size("member")
    vmem = pltpu.VMEM
    dma = pltpu.SemaphoreType.DMA

    def body(*refs):
        step_kernel(members, *refs)

    out = pl.pallas_call(
        body,
        name="decoder_step",
        out_shape=jax.ShapeDtypeStruct((32, 1024), F32),
        in_specs=[pl.BlockSpec(memory_space=pl.ANY)] * 11,
        out_specs=pl.BlockSpec(memory_space=pltpu.VMEM),
        scratch_shapes=[
            vmem((8, 16, 1024), BF16),
            vmem((3, 1, 768), jnp.int32),
            vmem((3, 1, 768), F32),
            vmem((112, 768), F32),
            vmem((12, 1, 112), F32),
            vmem((1, 12), F32),
            vmem((1, 112), F32),
            vmem((1, 112), F32),
            vmem((1024, 1024), BF16),
            vmem((1, 1024), F32),
            vmem((128, 1024), BF16),
            vmem((768, 128), F32),
            vmem((16, 128), F32),
            vmem((16, 128), F32),
            vmem((768, 384), BF16),
            vmem((128, 768), BF16),
            vmem((768, 1024), F32),
            vmem((768, 1024), F32),
            vmem((768, 1152), BF16),
            vmem((128, 1152), F32),
            vmem((64, 8, 128), F32),
            vmem((64, 4, 128), F32),
            vmem((64, 8, 128), F32),
            vmem((64, 4, 128), F32),
            vmem((32, 8, 128), F32),
            vmem((64, 8, 128), F32),
            vmem((32, 8, 128), F32),
            vmem((64, 8, 128), BF16),
            vmem((64, 4, 128), BF16),
            vmem((64, 8, 128), BF16),
            vmem((64, 4, 128), BF16),
            vmem((8, 16, 1024), F32),
            vmem((8, 16, 1024), BF16),
            vmem((2, 16, 1024), BF16),
            vmem((6, 16, 1024), BF16),
            dma((11,)),
            pltpu.SemaphoreType.REGULAR((3,)),
            dma((6,)),
            dma((6,)),
            dma((2,)),
            dma((2,)),
            dma((2,)),
            dma((2,)),
            dma((6,)),
            dma((6,)),
        ],
        compiler_params=pltpu.CompilerParams(collective_id=0, has_side_effects=True),
    )(
        processor_latent.reshape(2, 16, 1024),
        jnp.transpose(stencil_index, (1, 0, 2)),
        jnp.transpose(interp_weight, (1, 0, 2)),
        prev_state[0],
        jnp.transpose(observed, (2, 0, 1)),
        cell_area,
        var_weight.reshape(1, -1),
        hidden_weight,
        hidden_bias.reshape(1, -1),
        output_weight.T,
        output_bias.reshape(1, -1),
    )
    return out[None]


def solution(mesh):
    in_specs = (
        P("member", "shard", None),
        P("shard", None, None),
        P("shard", None, None),
        P("shard", None, None),
        P("shard", None, "member"),
        P("shard", "member"),
        P(),
        P(),
        P(),
        P(),
        P(),
    )
    out_specs = P("member", "shard", None)
    return jax.shard_map(local, mesh=mesh, in_specs=in_specs, out_specs=out_specs, check_vma=False)
```

```python
import jax
import jax.numpy as jnp
from jax import lax
from jax.experimental import pallas as pl
from jax.experimental.pallas import tpu as pltpu
from jax.sharding import PartitionSpec as P

smoothing = 0.05
fairness = 0.95
epsilon = 1e-05

MESH_ID = pl.DeviceIdType.MESH
F32 = jnp.float32
BF16 = jnp.bfloat16
NN = (((1,), (0,)), ((), ()))
NT = (((1,), (1,)), ((), ()))
VARS = 112


def slope(differ):
    return differ * lax.rsqrt(differ * differ + smoothing * smoothing)


def dot(a, b, dims, precision=None):
    return lax.dot_general(a, b, dims, precision=precision, preferred_element_type=F32)


def split(value):
    high = value.astype(BF16)
    return high, (value - high.astype(F32)).astype(BF16)


def ring():
    spot = lax.axis_index("shard")
    return spot, lax.rem(spot + 1, 4), lax.rem(spot + 3, 4), lax.rem(spot + 2, 4)


def signal(barrier, axis, to):
    pl.semaphore_signal(barrier, inc=1, device_id={axis: to}, device_id_type=MESH_ID)


def member_lines(me):
    core = lax.rem(me, 2)
    y = lax.rem(lax.div(me, 2), 4)
    x = lax.rem(lax.div(me, 8), 4)
    z = lax.div(me, 32)
    x_line = [me + 8 * (lax.rem(x + step, 4) - x) for step in (1, 2, 3)]
    y_line = [me + 2 * (lax.rem(y + step, 4) - y) for step in (1, 2, 3)]
    return x_line, y_line, [me + 32 * (1 - 2 * z)], [me + 1 - 2 * core]


def step_kernel(
    members,
    mesh_in,
    stencil_in,
    weight_in,
    prev_in,
    observed_in,
    area_in,
    var_in,
    hidden_in,
    hidden_bias_in,
    output_in,
    output_bias_in,
    out_ref,
    gathered,
    stencil,
    weight,
    prev,
    observed,
    area,
    var,
    output_bias,
    hidden,
    hidden_bias,
    output,
    inverse_ref,
    stack,
    target,
    coefficient,
    blend,
    blend_t,
    product,
    slope_act,
    grad_side,
    joined,
    forecast_out_a,
    forecast_out_b,
    forecast_in_a,
    forecast_in_b,
    state_b,
    sums_a,
    sums_b,
    cot_out_a,
    cot_out_b,
    cot_in_a,
    cot_in_b,
    result_ref,
    part_out,
    part_hop,
    part_in,
    local_sem,
    known,
    gather_send,
    gather_recv,
    cast_send,
    cast_recv,
    back_send,
    back_recv,
    part_send,
    part_recv,
):
    me = lax.axis_index("member")
    spot, right, left, across = ring()
    lines = member_lines(me)
    barrier = pltpu.get_barrier_semaphore()
    for neighbour in (left, right):
        signal(barrier, "shard", neighbour)
    for line in lines:
        for peer in line:
            signal(barrier, "member", peer)
    loads = [
        pltpu.make_async_copy(source, place, local_sem.at[number])
        for number, (source, place) in enumerate(
            (
                (stencil_in, stencil),
                (weight_in, weight),
                (prev_in, prev),
                (observed_in, observed),
                (area_in, area),
                (var_in, var),
                (output_bias_in, output_bias),
                (mesh_in, gathered.at[pl.ds(2 * spot, 2)]),
                (hidden_in, hidden),
                (hidden_bias_in, hidden_bias),
                (output_in, output.at[pl.ds(0, VARS)]),
            )
        )
    ]
    for load in loads:
        load.start()
    pl.semaphore_wait(barrier, 10)
    for peer in lines[0]:
        signal(known.at[0], "member", peer)

    def copy(number, source, slot, to):
        return pltpu.make_async_remote_copy(
            src_ref=source,
            dst_ref=gathered.at[slot],
            send_sem=gather_send.at[number],
            recv_sem=gather_recv.at[number],
            device_id={"shard": to},
            device_id_type=MESH_ID,
        )

    own = [
        copy(0, mesh_in.at[0], 2 * spot, right),
        copy(1, mesh_in.at[1], 2 * spot + 1, left),
        copy(2, mesh_in.at[1], 2 * spot + 1, right),
        copy(3, mesh_in.at[0], 2 * spot, left),
    ]
    for each in own:
        each.start()
    for load in loads[:7]:
        load.wait()

    row_ids = lax.broadcasted_iota(jnp.int32, (128, 768), 0)
    cells_t = jnp.zeros((128, 768), F32)
    for k in range(3):
        cells_t = cells_t + jnp.where(stencil[k] == row_ids, weight[k], 0.0)
    natural = lax.broadcasted_iota(jnp.int32, (768, 768), 1)
    place = lax.broadcasted_iota(jnp.int32, (768, 768), 0)
    cell_of = jnp.where(
        place < 512,
        lax.shift_right_logical(place, 3) * 12 + (place & 7),
        lax.shift_right_logical(place - 512, 2) * 12 + 8 + (place & 3),
    )
    order = jnp.where(natural == cell_of, 1.0, 0.0).astype(BF16)
    cells_high = cells_t.astype(BF16)
    ordered = dot(order, cells_high, NT).astype(BF16)
    blend[:, :128] = ordered
    blend[:, 128:] = ordered
    blend_t[...] = dot(cells_high, order, NT).astype(BF16)

    slots = lax.broadcasted_iota(jnp.int32, (16, 768), 0)
    slots = jnp.where(slots < 12, slots, slots - 4)
    chosen = jnp.where(
        lax.broadcasted_iota(jnp.int32, (16, 768), 1) == slots + 12 * me, 1.0, 0.0
    ).astype(F32)
    target[...] = jnp.zeros((16, 128), F32)
    for slot in range(16):
        cell = slot if slot < 12 else slot - 4
        target[slot : slot + 1, :VARS] = observed[cell] - output_bias[...]
    target[:, :VARS] = target[:, :VARS] - dot(chosen, prev[...], NT, lax.Precision.HIGHEST)
    lanes = lax.broadcasted_iota(jnp.int32, (16, 12), 1)
    cell_ids = lax.broadcasted_iota(jnp.int32, (16, 12), 0)
    cell_ids = jnp.where(cell_ids < 12, cell_ids, cell_ids - 4)
    area_column = jnp.sum(
        jnp.where(lanes == cell_ids, area[...], 0.0), axis=1, keepdims=True
    )
    coefficient[...] = jnp.zeros((16, 128), F32)
    coefficient[:, :VARS] = area_column * var[...]

    pl.semaphore_wait(known.at[0], 3)
    for peer in lines[1]:
        signal(known.at[1], "member", peer)
    own[0].wait_recv()
    relay_right = copy(4, gathered.at[2 * left], 2 * left, right)
    relay_right.start()
    own[1].wait_recv()
    relay_left = copy(5, gathered.at[2 * right + 1], 2 * right + 1, left)
    relay_left.start()
    pl.semaphore_wait(known.at[1], 3)
    for peer in lines[2]:
        signal(known.at[2], "member", peer)
    output[VARS:] = jnp.zeros((128 - VARS, 1024), BF16)
    for load in loads[7:]:
        load.wait()
    for each in own[2:] + [relay_right, relay_left]:
        each.wait_recv()

    rows_low = gathered[...].reshape(128, 1024)
    rows = rows_low.astype(F32)
    average = jnp.mean(rows, axis=1, keepdims=True)
    row_high, row_low = split(rows - average)
    cross = dot(row_low, row_high, NT)
    gram = (dot(row_high, row_high, NT) + cross + cross.T) * (1.0 / 1024)
    through_all = dot(
        jnp.concatenate([rows_low, jnp.ones((16, 1024), BF16)], axis=0), hidden[...], NN
    )
    through = through_all[:128] - average * through_all[128:129]
    through_high, through_low = split(through)
    stack[:128, :1024] = through_high
    stack[128:, :1024] = through_low
    gram_high, gram_low = split(gram)
    stack[:128, 1024:] = gram_high
    stack[128:, 1024:] = gram_low

    def exchange(source, place, to, send, recv):
        return pltpu.make_async_remote_copy(
            src_ref=source.at[to],
            dst_ref=place.at[me],
            send_sem=send,
            recv_sem=recv,
            device_id={"member": to},
            device_id_type=MESH_ID,
        )

    def send_forecast(source, place, number, first, count, apart):
        def start(offset):
            to = first + lax.rem(me + 1 + offset, count)
            exchange(source, place, to, cast_send.at[number], cast_recv.at[number]).start()

        for offset in range(count - 1):
            start(offset)

        @pl.when(apart)
        def _():
            start(count - 1)

    def updates(span):
        raw = dot(blend[span], stack[...], NN)
        variance = jnp.sum(
            raw[:, 1024:] * blend[span, :128].astype(F32), axis=1, keepdims=True
        )
        inverse = lax.rsqrt(variance + epsilon)
        inverse_ref[span] = jnp.broadcast_to(inverse, (128, 128))
        value = raw[:, :1024] * inverse
        product[span] = value
        act = value + hidden_bias[...]
        active = act * (0.5 * jnp.tanh(0.5 * act) + 0.5)
        return dot(active.astype(BF16), output[...], NT)

    pl.semaphore_wait(known.at[2], 1)

    @pl.loop(0, 4)
    def _(step):
        part = lax.rem(lax.div(me, 16) + 1 + step, 4)
        update = updates(pl.ds(pl.multiple_of(part * 128, 128), 128))
        forecast_out_a[pl.ds(part * 16, 16)] = update.reshape(16, 8, 128)
        send_forecast(forecast_out_a, forecast_in_a, 0, part * 16, 16, step < 3)

    @pl.loop(0, 2)
    def _(step):
        part = lax.rem(lax.div(me, 32) + 1 + step, 2)
        update = updates(pl.ds(pl.multiple_of(512 + part * 128, 128), 128))
        for piece in range(32):
            forecast_out_b[part * 32 + piece] = update[piece * 4 : piece * 4 + 4]
        send_forecast(forecast_out_b, forecast_in_b, 1, part * 32, 32, step < 1)

    forecast_in_a[me] = forecast_out_a[me]
    forecast_in_b[me] = forecast_out_b[me]

    @pl.loop(0, 6)
    def _(part):
        span = pl.ds(pl.multiple_of(part * 128, 128), 128)
        act = product[span] + hidden_bias[...]
        gate = 0.5 * jnp.tanh(0.5 * act) + 0.5
        slope_act[span] = gate * (1.0 + act * (1.0 - gate)) * inverse_ref[span][:, :1]

    others = pl.ds(0, members - 1)

    def settle(ref, sem):
        pltpu.make_async_copy(ref.at[others], ref.at[others], sem).wait()

    settle(forecast_in_a, cast_recv.at[0])

    @pl.loop(0, 8)
    def _(block):
        base = block * 8
        values = [forecast_in_a[base + i] for i in range(8)]
        totals = [jnp.zeros((8, 128), F32) for _ in range(8)]
        for i in range(8):
            for j in range(i + 1, 8):
                push = slope(values[i] - values[j])
                totals[i] = totals[i] + push
                totals[j] = totals[j] - push
        for i in range(8):
            sums_a[base + i] = totals[i]

    @pl.loop(0, 28)
    def _(step):
        first = lax.rem(step, 8) * 8
        second = lax.rem(lax.rem(step, 8) + lax.div(step, 8) + 1, 8) * 8
        values = [forecast_in_a[first + i] for i in range(8)]
        totals = [sums_a[first + i] for i in range(8)]
        for j in range(8):
            other = forecast_in_a[second + j]
            total = sums_a[second + j]
            for i in range(8):
                push = slope(values[i] - other)
                totals[i] = totals[i] + push
                total = total - push
            sums_a[second + j] = total
        for i in range(8):
            sums_a[first + i] = totals[i]

    pair_factor = (1.0 - (1.0 - fairness) / members) / (members - 1)

    @pl.loop(0, 8)
    def _(block):
        for i in range(8):
            m = block * 8 + i
            cot_out_a[m] = (
                coefficient[:8]
                * (slope(forecast_in_a[m] - target[:8]) - pair_factor * sums_a[m])
            ).astype(BF16)

    core = lax.rem(me, 2)
    row_y = lax.rem(lax.div(me, 2), 4)
    row_x = lax.rem(lax.div(me, 8), 4)
    row_z = lax.div(me, 32)
    xs = [8 * lax.rem(row_x + step, 4) for step in range(4)]
    ys = [2 * lax.rem(row_y + step, 4) for step in range(4)]
    zs = [32 * row_z, 32 * (1 - row_z)]
    cs = [core, 1 - core]
    moves = [
        (z + min(x, 4 - x) + min(y, 4 - y), z, x, y, c)
        for z in range(2)
        for x in range(4)
        for y in range(4)
        for c in range(2)
        if z + x + y + c
    ]
    moves.sort(key=lambda move: -move[0])

    def send_back(source, place, number):
        for _, z, x, y, c in moves:
            to = zs[z] + xs[x] + ys[y] + cs[c]
            exchange(source, place, to, back_send.at[number], back_recv.at[number]).start()

    send_back(cot_out_a, cot_in_a, 0)
    cot_in_a[me] = cot_out_a[me]

    settle(forecast_in_b, cast_recv.at[1])
    for m in range(32):
        state_b[m] = jnp.concatenate([forecast_in_b[m], forecast_in_b[m + 32]], axis=0)

    def half_turn(value):
        return pltpu.roll(value, 4, 0)

    @pl.loop(0, 4)
    def _(block):
        base = block * 8
        values = [state_b[base + i] for i in range(8)]
        turned = [half_turn(value) for value in values]
        totals = [slope(values[i] - turned[i]) for i in range(8)]
        crossed = [jnp.zeros((8, 128), F32) for _ in range(8)]
        for i in range(8):
            for j in range(i + 1, 8):
                push = slope(values[i] - values[j])
                totals[i] = totals[i] + push
                totals[j] = totals[j] - push
                push = slope(values[i] - turned[j])
                totals[i] = totals[i] + push
                crossed[j] = crossed[j] - push
        for i in range(8):
            sums_b[base + i] = totals[i] + half_turn(crossed[i])

    @pl.loop(0, 6)
    def _(step):
        first = lax.rem(step, 4) * 8
        second = lax.rem(lax.rem(step, 4) + lax.div(step, 4) + 1, 4) * 8
        values = [state_b[first + i] for i in range(8)]
        totals = [sums_b[first + i] for i in range(8)]
        for j in range(8):
            other = state_b[second + j]
            turned = half_turn(other)
            total = sums_b[second + j]
            crossed = jnp.zeros((8, 128), F32)
            for i in range(8):
                push = slope(values[i] - other)
                totals[i] = totals[i] + push
                total = total - push
                push = slope(values[i] - turned)
                totals[i] = totals[i] + push
                crossed = crossed - push
            sums_b[second + j] = total + half_turn(crossed)
        for i in range(8):
            sums_b[first + i] = totals[i]

    @pl.loop(0, 8)
    def _(block):
        for i in range(4):
            m = block * 4 + i
            cot = coefficient[8:] * (
                slope(state_b[m] - target[8:]) - pair_factor * sums_b[m]
            )
            cot_out_b[m] = cot[:4].astype(BF16)
            cot_out_b[m + 32] = cot[4:].astype(BF16)

    send_back(cot_out_b, cot_in_b, 1)
    cot_in_b[me] = cot_out_b[me]

    def backward(cot, span):
        grad = dot(cot, output[...], NN) * slope_act[span]
        grad_side[span, :1024] = grad.astype(BF16)
        along = jnp.sum(grad * product[span], axis=1, keepdims=True) * (1.0 / 1024)
        grad_side[span, 1024:] = (
            blend[span, :128].astype(F32) * (inverse_ref[span] * along)
        ).astype(BF16)

    settle(cot_in_a, back_recv.at[0])

    @pl.loop(0, 4)
    def _(part):
        cot = cot_in_a[pl.ds(part * 16, 16)].astype(F32).reshape(128, 128).astype(BF16)
        backward(cot, pl.ds(pl.multiple_of(part * 128, 128), 128))

    joined[...] = dot(blend_t[:, :512], grad_side[:512], NN)
    settle(cot_in_b, back_recv.at[1])

    @pl.loop(0, 2)
    def _(part):
        cot = jnp.concatenate(
            [cot_in_b[part * 32 + piece].astype(F32) for piece in range(32)], axis=0
        ).astype(BF16)
        backward(cot, pl.ds(pl.multiple_of(512 + part * 128, 128), 128))

    total = joined[...] + dot(blend_t[:, 512:], grad_side[512:], NN)
    outer = total[:, :1024].astype(BF16)
    inner = total[:, 1024:].astype(BF16)
    result = dot(outer, hidden[...], NT)
    result = result - dot(inner, gathered[...].reshape(128, 1024), NN)
    result = result - jnp.mean(result, axis=1, keepdims=True)
    result_ref[...] = result.reshape(8, 16, 1024)
    part_out[...] = result.astype(BF16).reshape(8, 16, 1024)

    def part_copy(number, source, to):
        return pltpu.make_async_remote_copy(
            src_ref=source,
            dst_ref=part_in.at[number],
            send_sem=part_send.at[number],
            recv_sem=part_recv.at[number],
            device_id={"shard": to},
            device_id_type=MESH_ID,
        )

    hops = [
        part_copy(0, part_out.at[2 * across], right),
        part_copy(1, part_out.at[2 * across + 1], left),
        part_copy(2, part_out.at[2 * right + 1], right),
        part_copy(3, part_out.at[2 * left], left),
        part_copy(4, part_hop.at[0], right),
        part_copy(5, part_hop.at[1], left),
    ]
    for hop in hops[:4]:
        hop.start()
    hops[0].wait_recv()
    part_hop[0] = (part_in[0].astype(F32) + result_ref[2 * right]).astype(BF16)
    hops[4].start()
    hops[1].wait_recv()
    part_hop[1] = (part_in[1].astype(F32) + result_ref[2 * left + 1]).astype(BF16)
    hops[5].start()
    for hop in hops[2:]:
        hop.wait_recv()
    out_ref[:16] = result_ref[2 * spot] + part_in[4].astype(F32) + part_in[3].astype(F32)
    out_ref[16:] = result_ref[2 * spot + 1] + part_in[2].astype(F32) + part_in[5].astype(F32)

    for each in own + [relay_right, relay_left] + hops:
        each.wait_send()
    settle(forecast_out_a, cast_send.at[0])
    settle(forecast_out_b, cast_send.at[1])
    settle(cot_out_a, back_send.at[0])
    settle(cot_out_b, back_send.at[1])


def local(
    processor_latent,
    stencil_index,
    interp_weight,
    prev_state,
    observed,
    cell_area,
    var_weight,
    hidden_weight,
    hidden_bias,
    output_weight,
    output_bias,
):
    members = lax.axis_size("member")
    vmem = pltpu.VMEM
    dma = pltpu.SemaphoreType.DMA

    def body(*refs):
        step_kernel(members, *refs)

    out = pl.pallas_call(
        body,
        name="decoder_step",
        out_shape=jax.ShapeDtypeStruct((32, 1024), F32),
        in_specs=[pl.BlockSpec(memory_space=pl.ANY)] * 11,
        out_specs=pl.BlockSpec(memory_space=pltpu.VMEM),
        scratch_shapes=[
            vmem((8, 16, 1024), BF16),
            vmem((3, 1, 768), jnp.int32),
            vmem((3, 1, 768), F32),
            vmem((112, 768), F32),
            vmem((12, 1, 112), F32),
            vmem((1, 12), F32),
            vmem((1, 112), F32),
            vmem((1, 112), F32),
            vmem((1024, 1024), BF16),
            vmem((1, 1024), F32),
            vmem((128, 1024), BF16),
            vmem((768, 128), F32),
            vmem((256, 1152), BF16),
            vmem((16, 128), F32),
            vmem((16, 128), F32),
            vmem((768, 256), BF16),
            vmem((128, 768), BF16),
            vmem((768, 1024), F32),
            vmem((768, 1024), F32),
            vmem((768, 1152), BF16),
            vmem((128, 1152), F32),
            vmem((64, 8, 128), F32),
            vmem((64, 4, 128), F32),
            vmem((64, 8, 128), F32),
            vmem((64, 4, 128), F32),
            vmem((32, 8, 128), F32),
            vmem((64, 8, 128), F32),
            vmem((32, 8, 128), F32),
            vmem((64, 8, 128), BF16),
            vmem((64, 4, 128), BF16),
            vmem((64, 8, 128), BF16),
            vmem((64, 4, 128), BF16),
            vmem((8, 16, 1024), F32),
            vmem((8, 16, 1024), BF16),
            vmem((2, 16, 1024), BF16),
            vmem((6, 16, 1024), BF16),
            dma((11,)),
            pltpu.SemaphoreType.REGULAR((3,)),
            dma((6,)),
            dma((6,)),
            dma((2,)),
            dma((2,)),
            dma((2,)),
            dma((2,)),
            dma((6,)),
            dma((6,)),
        ],
        compiler_params=pltpu.CompilerParams(
            collective_id=0, has_side_effects=True, vmem_limit_bytes=40 << 20
        ),
    )(
        *(
            pltpu.with_memory_space_constraint(each, pltpu.MemorySpace.HBM)
            for each in (
                processor_latent.reshape(2, 16, 1024),
                jnp.transpose(stencil_index, (1, 0, 2)),
                jnp.transpose(interp_weight, (1, 0, 2)),
                prev_state[0],
                jnp.transpose(observed, (2, 0, 1)),
                cell_area,
                var_weight.reshape(1, -1),
                hidden_weight,
                hidden_bias.reshape(1, -1),
                output_weight.T,
                output_bias.reshape(1, -1),
            )
        )
    )
    return out[None]


def solution(mesh):
    in_specs = (
        P("member", "shard", None),
        P("shard", None, None),
        P("shard", None, None),
        P("shard", None, None),
        P("shard", None, "member"),
        P("shard", "member"),
        P(),
        P(),
        P(),
        P(),
        P(),
    )
    out_specs = P("member", "shard", None)
    return jax.shard_map(local, mesh=mesh, in_specs=in_specs, out_specs=out_specs, check_vma=False)
```

```python
import jax
import jax.numpy as jnp
from jax import lax
from jax.experimental import pallas as pl
from jax.experimental.pallas import tpu as pltpu
from jax.sharding import PartitionSpec as P

smoothing = 0.05
fairness = 0.95
epsilon = 1e-05

MESH_ID = pl.DeviceIdType.MESH
F32 = jnp.float32
BF16 = jnp.bfloat16
NN = (((1,), (0,)), ((), ()))
NT = (((1,), (1,)), ((), ()))
VARS = 112


def slope(differ):
    return differ * lax.rsqrt(differ * differ + smoothing * smoothing)


def dot(a, b, dims, precision=None):
    return lax.dot_general(a, b, dims, precision=precision, preferred_element_type=F32)


def split(value):
    high = value.astype(BF16)
    return high, (value - high.astype(F32)).astype(BF16)


def ring():
    spot = lax.axis_index("shard")
    return spot, lax.rem(spot + 1, 4), lax.rem(spot + 3, 4), lax.rem(spot + 2, 4)


def signal(barrier, axis, to):
    pl.semaphore_signal(barrier, inc=1, device_id={axis: to}, device_id_type=MESH_ID)


def member_lines(me):
    core = lax.rem(me, 2)
    y = lax.rem(lax.div(me, 2), 4)
    x = lax.rem(lax.div(me, 8), 4)
    z = lax.div(me, 32)
    x_line = [me + 8 * (lax.rem(x + step, 4) - x) for step in (1, 2, 3)]
    y_line = [me + 2 * (lax.rem(y + step, 4) - y) for step in (1, 2, 3)]
    return x_line, y_line, [me + 32 * (1 - 2 * z)], [me + 1 - 2 * core]


def step_kernel(
    members,
    mesh_in,
    stencil_in,
    weight_in,
    prev_in,
    observed_in,
    area_in,
    var_in,
    hidden_in,
    hidden_bias_in,
    output_in,
    output_bias_in,
    out_ref,
    gathered,
    stencil,
    weight,
    prev,
    observed,
    area,
    var,
    output_bias,
    hidden,
    hidden_bias,
    output,
    inverse_ref,
    stack,
    target,
    coefficient,
    blend,
    blend_t,
    product,
    slope_act,
    grad_side,
    joined,
    forecast_out_a,
    forecast_out_b,
    forecast_in_a,
    forecast_in_b,
    state_b,
    sums_a,
    sums_b,
    cot_out_a,
    cot_out_b,
    cot_in_a,
    cot_in_b,
    result_ref,
    part_out,
    part_hop,
    part_in,
    local_sem,
    known,
    gather_send,
    gather_recv,
    cast_send,
    cast_recv,
    back_send,
    back_recv,
    part_send,
    part_recv,
):
    me = lax.axis_index("member")
    spot, right, left, across = ring()
    lines = member_lines(me)
    barrier = pltpu.get_barrier_semaphore()
    for neighbour in (left, right):
        signal(barrier, "shard", neighbour)
    for line in lines:
        for peer in line:
            signal(barrier, "member", peer)
    loads = [
        pltpu.make_async_copy(source, place, local_sem.at[number])
        for number, (source, place) in enumerate(
            (
                (stencil_in, stencil),
                (weight_in, weight),
                (prev_in, prev),
                (observed_in, observed),
                (area_in, area),
                (var_in, var),
                (output_bias_in, output_bias),
                (mesh_in, gathered.at[pl.ds(2 * spot, 2)]),
                (hidden_in, hidden),
                (hidden_bias_in, hidden_bias),
                (output_in, output.at[pl.ds(0, VARS)]),
            )
        )
    ]
    pl.semaphore_wait(barrier, 10)
    for peer in lines[0]:
        signal(known.at[0], "member", peer)

    def copy(number, source, slot, to):
        return pltpu.make_async_remote_copy(
            src_ref=source,
            dst_ref=gathered.at[slot],
            send_sem=gather_send.at[number],
            recv_sem=gather_recv.at[number],
            device_id={"shard": to},
            device_id_type=MESH_ID,
        )

    own = [
        copy(0, mesh_in.at[0], 2 * spot, right),
        copy(1, mesh_in.at[1], 2 * spot + 1, left),
        copy(2, mesh_in.at[1], 2 * spot + 1, right),
        copy(3, mesh_in.at[0], 2 * spot, left),
    ]
    for each in own:
        each.start()
    for load in loads:
        load.start()
    for load in loads[:7]:
        load.wait()

    row_ids = lax.broadcasted_iota(jnp.int32, (128, 768), 0)
    cells_t = jnp.zeros((128, 768), F32)
    for k in range(3):
        cells_t = cells_t + jnp.where(stencil[k] == row_ids, weight[k], 0.0)
    natural = lax.broadcasted_iota(jnp.int32, (768, 768), 1)
    place = lax.broadcasted_iota(jnp.int32, (768, 768), 0)
    slot = jnp.where(
        place < 512,
        lax.shift_right_logical(place, 3),
        lax.shift_right_logical(place - 512, 2),
    )
    scorer = 2 * (slot & 31) + lax.shift_right_logical(slot, 5)
    cell_of = scorer * 12 + jnp.where(place < 512, place & 7, 8 + (place & 3))
    order = jnp.where(natural == cell_of, 1.0, 0.0).astype(BF16)
    cells_high = cells_t.astype(BF16)
    ordered = dot(order, cells_high, NT).astype(BF16)
    blend[:, :128] = ordered
    blend[:, 128:] = ordered
    blend_t[...] = dot(cells_high, order, NT).astype(BF16)

    slots = lax.broadcasted_iota(jnp.int32, (16, 768), 0)
    slots = jnp.where(slots < 12, slots, slots - 4)
    chosen = jnp.where(
        lax.broadcasted_iota(jnp.int32, (16, 768), 1) == slots + 12 * me, 1.0, 0.0
    ).astype(F32)
    target[...] = jnp.zeros((16, 128), F32)
    for slot in range(16):
        cell = slot if slot < 12 else slot - 4
        target[slot : slot + 1, :VARS] = observed[cell] - output_bias[...]
    target[:, :VARS] = target[:, :VARS] - dot(chosen, prev[...], NT, lax.Precision.HIGHEST)
    lanes = lax.broadcasted_iota(jnp.int32, (16, 12), 1)
    cell_ids = lax.broadcasted_iota(jnp.int32, (16, 12), 0)
    cell_ids = jnp.where(cell_ids < 12, cell_ids, cell_ids - 4)
    area_column = jnp.sum(
        jnp.where(lanes == cell_ids, area[...], 0.0), axis=1, keepdims=True
    )
    coefficient[...] = jnp.zeros((16, 128), F32)
    coefficient[:, :VARS] = area_column * var[...]

    pl.semaphore_wait(known.at[0], 3)
    for peer in lines[1]:
        signal(known.at[1], "member", peer)
    own[0].wait_recv()
    relay_right = copy(4, gathered.at[2 * left], 2 * left, right)
    relay_right.start()
    own[1].wait_recv()
    relay_left = copy(5, gathered.at[2 * right + 1], 2 * right + 1, left)
    relay_left.start()
    pl.semaphore_wait(known.at[1], 3)
    for peer in lines[2]:
        signal(known.at[2], "member", peer)
    output[VARS:] = jnp.zeros((128 - VARS, 1024), BF16)
    for load in loads[7:]:
        load.wait()
    for each in own[2:] + [relay_right, relay_left]:
        each.wait_recv()

    rows_low = gathered[...].reshape(128, 1024)
    rows = rows_low.astype(F32)
    average = jnp.mean(rows, axis=1, keepdims=True)
    row_high, row_low = split(rows - average)
    cross = dot(row_low, row_high, NT)
    gram = (dot(row_high, row_high, NT) + cross + cross.T) * (1.0 / 1024)
    through_all = dot(
        jnp.concatenate([rows_low, jnp.ones((16, 1024), BF16)], axis=0), hidden[...], NN
    )
    through = through_all[:128] - average * through_all[128:129]
    through_high, through_low = split(through)
    stack[:128, :1024] = through_high
    stack[128:, :1024] = through_low
    gram_high, gram_low = split(gram)
    stack[:128, 1024:] = gram_high
    stack[128:, 1024:] = gram_low

    core = lax.rem(me, 2)
    chip = lax.div(me, 2)
    my_slot = core * 32 + chip
    row_y = lax.rem(chip, 4)
    row_x = lax.rem(lax.div(chip, 4), 4)
    row_z = lax.div(chip, 16)
    xs = [4 * lax.rem(row_x + step, 4) for step in range(4)]
    ys = [lax.rem(row_y + step, 4) for step in range(4)]
    zs = [16 * row_z, 16 * (1 - row_z)]
    moves = [
        (z + min(x, 4 - x) + min(y, 4 - y), z, x, y)
        for z in range(2)
        for x in range(4)
        for y in range(4)
        if z + x + y
    ]
    moves.sort(key=lambda move: -move[0])
    chips = [zs[z] + xs[x] + ys[y] for _, z, x, y in moves]

    def exchange(source, source_slot, place, place_slot, to, send, recv):
        pltpu.make_async_remote_copy(
            src_ref=source.at[source_slot],
            dst_ref=place.at[place_slot],
            send_sem=send,
            recv_sem=recv,
            device_id={"member": to},
            device_id_type=MESH_ID,
        ).start()

    def send_forecast(source, place, number, sides):
        def start(other, side):
            exchange(
                source,
                side * 32 + other,
                place,
                me,
                2 * other + side,
                cast_send.at[number],
                cast_recv.at[number],
            )

        for other in chips:
            for side in sides:
                start(other, side)
        if len(sides) == 2:
            start(chip, 1 - core)
        else:

            @pl.when(core != sides[0])
            def _():
                start(chip, sides[0])

    def updates(span):
        raw = dot(blend[span], stack[...], NN)
        variance = jnp.sum(
            raw[:, 1024:] * blend[span, :128].astype(F32), axis=1, keepdims=True
        )
        inverse = lax.rsqrt(variance + epsilon)
        inverse_ref[span] = jnp.broadcast_to(inverse, (256, 128))
        value = raw[:, :1024] * inverse
        product[span] = value
        act = value + hidden_bias[...]
        active = act * (0.5 * jnp.tanh(0.5 * act) + 0.5)
        return dot(active.astype(BF16), output[...], NT)

    pl.semaphore_wait(known.at[2], 1)

    for side in range(2):
        update = updates(pl.ds(side * 256, 256))
        forecast_out_a[pl.ds(side * 32, 32)] = update.reshape(32, 8, 128)
        send_forecast(forecast_out_a, forecast_in_a, 0, (side,))

    update = updates(pl.ds(512, 256))
    for piece in range(64):
        forecast_out_b[piece] = update[piece * 4 : piece * 4 + 4]
    send_forecast(forecast_out_b, forecast_in_b, 1, (0, 1))

    forecast_in_a[me] = forecast_out_a[my_slot]
    forecast_in_b[me] = forecast_out_b[my_slot]

    @pl.loop(0, 6)
    def _(part):
        span = pl.ds(pl.multiple_of(part * 128, 128), 128)
        act = product[span] + hidden_bias[...]
        gate = 0.5 * jnp.tanh(0.5 * act) + 0.5
        slope_act[span] = gate * (1.0 + act * (1.0 - gate)) * inverse_ref[span][:, :1]

    others = pl.ds(0, members - 1)

    def settle(ref, sem):
        pltpu.make_async_copy(ref.at[others], ref.at[others], sem).wait()

    settle(forecast_in_a, cast_recv.at[0])

    @pl.loop(0, 8)
    def _(block):
        base = block * 8
        values = [forecast_in_a[base + i] for i in range(8)]
        totals = [jnp.zeros((8, 128), F32) for _ in range(8)]
        for i in range(8):
            for j in range(i + 1, 8):
                push = slope(values[i] - values[j])
                totals[i] = totals[i] + push
                totals[j] = totals[j] - push
        for i in range(8):
            sums_a[base + i] = totals[i]

    def pair_blocks(first, seconds):
        values = [forecast_in_a[first + i] for i in range(8)]
        totals = [sums_a[first + i] for i in range(8)]
        for second in seconds:
            for j in range(8):
                other = forecast_in_a[second + j]
                total = sums_a[second + j]
                for i in range(8):
                    push = slope(values[i] - other)
                    totals[i] = totals[i] + push
                    total = total - push
                sums_a[second + j] = total
        for i in range(8):
            sums_a[first + i] = totals[i]

    @pl.loop(0, 12)
    def _(step):
        block = lax.rem(step, 8)
        apart = block + 1 + 2 * lax.div(step, 8)
        pair_blocks(block * 8, (lax.rem(apart, 8) * 8, lax.rem(apart + 1, 8) * 8))

    @pl.loop(4, 8)
    def _(block):
        pair_blocks(block * 8, (lax.rem(block + 3, 8) * 8,))

    pair_factor = (1.0 - (1.0 - fairness) / members) / (members - 1)

    @pl.loop(0, 8)
    def _(block):
        for i in range(8):
            m = block * 8 + i
            cot_out_a[m] = (
                coefficient[:8]
                * (slope(forecast_in_a[m] - target[:8]) - pair_factor * sums_a[m])
            ).astype(BF16)

    def send_back(source, place, number):
        def start(to):
            exchange(source, to, place, my_slot, to, back_send.at[number], back_recv.at[number])

        for other in chips:
            for side in range(2):
                start(2 * other + side)
        start(2 * chip + 1 - core)

    send_back(cot_out_a, cot_in_a, 0)
    cot_in_a[my_slot] = cot_out_a[me]

    settle(forecast_in_b, cast_recv.at[1])
    for m in range(32):
        state_b[m] = jnp.concatenate([forecast_in_b[m], forecast_in_b[m + 32]], axis=0)

    def half_turn(value):
        return pltpu.roll(value, 4, 0)

    @pl.loop(0, 4)
    def _(block):
        base = block * 8
        values = [state_b[base + i] for i in range(8)]
        turned = [half_turn(value) for value in values]
        totals = [slope(values[i] - turned[i]) for i in range(8)]
        crossed = [jnp.zeros((8, 128), F32) for _ in range(8)]
        for i in range(8):
            for j in range(i + 1, 8):
                push = slope(values[i] - values[j])
                totals[i] = totals[i] + push
                totals[j] = totals[j] - push
                push = slope(values[i] - turned[j])
                totals[i] = totals[i] + push
                crossed[j] = crossed[j] - push
        for i in range(8):
            sums_b[base + i] = totals[i] + half_turn(crossed[i])

    @pl.loop(0, 6)
    def _(step):
        first = lax.rem(step, 4) * 8
        second = lax.rem(lax.rem(step, 4) + lax.div(step, 4) + 1, 4) * 8
        values = [state_b[first + i] for i in range(8)]
        totals = [sums_b[first + i] for i in range(8)]
        for j in range(8):
            other = state_b[second + j]
            turned = half_turn(other)
            total = sums_b[second + j]
            crossed = jnp.zeros((8, 128), F32)
            for i in range(8):
                push = slope(values[i] - other)
                totals[i] = totals[i] + push
                total = total - push
                push = slope(values[i] - turned)
                totals[i] = totals[i] + push
                crossed = crossed - push
            sums_b[second + j] = total + half_turn(crossed)
        for i in range(8):
            sums_b[first + i] = totals[i]

    @pl.loop(0, 8)
    def _(block):
        for i in range(4):
            m = block * 4 + i
            cot = coefficient[8:] * (
                slope(state_b[m] - target[8:]) - pair_factor * sums_b[m]
            )
            cot_out_b[m] = cot[:4].astype(BF16)
            cot_out_b[m + 32] = cot[4:].astype(BF16)

    send_back(cot_out_b, cot_in_b, 1)
    cot_in_b[my_slot] = cot_out_b[me]

    def backward(cot, span):
        grad = dot(cot, output[...], NN) * slope_act[span]
        grad_side[span, :1024] = grad.astype(BF16)
        along = jnp.sum(grad * product[span], axis=1, keepdims=True) * (1.0 / 1024)
        grad_side[span, 1024:] = (
            blend[span, :128].astype(F32) * (inverse_ref[span] * along)
        ).astype(BF16)

    settle(cot_in_a, back_recv.at[0])

    @pl.loop(0, 4)
    def _(part):
        cot = cot_in_a[pl.ds(part * 16, 16)].astype(F32).reshape(128, 128).astype(BF16)
        backward(cot, pl.ds(pl.multiple_of(part * 128, 128), 128))

    joined[...] = dot(blend_t[:, :512], grad_side[:512], NN)
    settle(cot_in_b, back_recv.at[1])

    @pl.loop(0, 2)
    def _(part):
        cot = jnp.concatenate(
            [cot_in_b[part * 32 + piece].astype(F32) for piece in range(32)], axis=0
        ).astype(BF16)
        backward(cot, pl.ds(pl.multiple_of(512 + part * 128, 128), 128))

    total = joined[...] + dot(blend_t[:, 512:], grad_side[512:], NN)
    outer = total[:, :1024].astype(BF16)
    inner = total[:, 1024:].astype(BF16)
    result = dot(outer, hidden[...], NT)
    result = result - dot(inner, gathered[...].reshape(128, 1024), NN)
    result = result - jnp.mean(result, axis=1, keepdims=True)
    result_ref[...] = result.reshape(8, 16, 1024)
    part_out[...] = result.astype(BF16).reshape(8, 16, 1024)

    def part_copy(number, source, to):
        return pltpu.make_async_remote_copy(
            src_ref=source,
            dst_ref=part_in.at[number],
            send_sem=part_send.at[number],
            recv_sem=part_recv.at[number],
            device_id={"shard": to},
            device_id_type=MESH_ID,
        )

    hops = [
        part_copy(0, part_out.at[2 * across], right),
        part_copy(1, part_out.at[2 * across + 1], left),
        part_copy(2, part_out.at[2 * right + 1], right),
        part_copy(3, part_out.at[2 * left], left),
        part_copy(4, part_hop.at[0], right),
        part_copy(5, part_hop.at[1], left),
    ]
    for hop in hops[:4]:
        hop.start()
    hops[0].wait_recv()
    part_hop[0] = (part_in[0].astype(F32) + result_ref[2 * right]).astype(BF16)
    hops[4].start()
    hops[1].wait_recv()
    part_hop[1] = (part_in[1].astype(F32) + result_ref[2 * left + 1]).astype(BF16)
    hops[5].start()
    for hop in hops[2:]:
        hop.wait_recv()
    out_ref[:16] = result_ref[2 * spot] + part_in[4].astype(F32) + part_in[3].astype(F32)
    out_ref[16:] = result_ref[2 * spot + 1] + part_in[2].astype(F32) + part_in[5].astype(F32)

    for each in own + [relay_right, relay_left] + hops:
        each.wait_send()
    settle(forecast_out_a, cast_send.at[0])
    settle(forecast_out_b, cast_send.at[1])
    settle(cot_out_a, back_send.at[0])
    settle(cot_out_b, back_send.at[1])


def local(
    processor_latent,
    stencil_index,
    interp_weight,
    prev_state,
    observed,
    cell_area,
    var_weight,
    hidden_weight,
    hidden_bias,
    output_weight,
    output_bias,
):
    members = lax.axis_size("member")
    vmem = pltpu.VMEM
    dma = pltpu.SemaphoreType.DMA

    def body(*refs):
        step_kernel(members, *refs)

    out = pl.pallas_call(
        body,
        name="decoder_step",
        out_shape=jax.ShapeDtypeStruct((32, 1024), F32),
        in_specs=[pl.BlockSpec(memory_space=pl.ANY)] * 11,
        out_specs=pl.BlockSpec(memory_space=pltpu.VMEM),
        scratch_shapes=[
            vmem((8, 16, 1024), BF16),
            vmem((3, 1, 768), jnp.int32),
            vmem((3, 1, 768), F32),
            vmem((112, 768), F32),
            vmem((12, 1, 112), F32),
            vmem((1, 12), F32),
            vmem((1, 112), F32),
            vmem((1, 112), F32),
            vmem((1024, 1024), BF16),
            vmem((1, 1024), F32),
            vmem((128, 1024), BF16),
            vmem((768, 128), F32),
            vmem((256, 1152), BF16),
            vmem((16, 128), F32),
            vmem((16, 128), F32),
            vmem((768, 256), BF16),
            vmem((128, 768), BF16),
            vmem((768, 1024), F32),
            vmem((768, 1024), F32),
            vmem((768, 1152), BF16),
            vmem((128, 1152), F32),
            vmem((64, 8, 128), F32),
            vmem((64, 4, 128), F32),
            vmem((64, 8, 128), F32),
            vmem((64, 4, 128), F32),
            vmem((32, 8, 128), F32),
            vmem((64, 8, 128), F32),
            vmem((32, 8, 128), F32),
            vmem((64, 8, 128), BF16),
            vmem((64, 4, 128), BF16),
            vmem((64, 8, 128), BF16),
            vmem((64, 4, 128), BF16),
            vmem((8, 16, 1024), F32),
            vmem((8, 16, 1024), BF16),
            vmem((2, 16, 1024), BF16),
            vmem((6, 16, 1024), BF16),
            dma((11,)),
            pltpu.SemaphoreType.REGULAR((3,)),
            dma((6,)),
            dma((6,)),
            dma((2,)),
            dma((2,)),
            dma((2,)),
            dma((2,)),
            dma((6,)),
            dma((6,)),
        ],
        compiler_params=pltpu.CompilerParams(
            collective_id=0, has_side_effects=True, vmem_limit_bytes=40 << 20
        ),
    )(
        *(
            pltpu.with_memory_space_constraint(each, pltpu.MemorySpace.HBM)
            for each in (
                processor_latent.reshape(2, 16, 1024),
                jnp.transpose(stencil_index, (1, 0, 2)),
                jnp.transpose(interp_weight, (1, 0, 2)),
                prev_state[0],
                jnp.transpose(observed, (2, 0, 1)),
                cell_area,
                var_weight.reshape(1, -1),
                hidden_weight,
                hidden_bias.reshape(1, -1),
                output_weight.T,
                output_bias.reshape(1, -1),
            )
        )
    )
    return out[None]


def solution(mesh):
    in_specs = (
        P("member", "shard", None),
        P("shard", None, None),
        P("shard", None, None),
        P("shard", None, None),
        P("shard", None, "member"),
        P("shard", "member"),
        P(),
        P(),
        P(),
        P(),
        P(),
    )
    out_specs = P("member", "shard", None)
    return jax.shard_map(local, mesh=mesh, in_specs=in_specs, out_specs=out_specs, check_vma=False)
```

```python
import jax
import jax.numpy as jnp
from jax import lax
from jax.experimental import pallas as pl
from jax.experimental.pallas import tpu as pltpu
from jax.sharding import PartitionSpec as P

smoothing = 0.05
fairness = 0.95
epsilon = 1e-05

MESH_ID = pl.DeviceIdType.MESH
F32 = jnp.float32
BF16 = jnp.bfloat16
NN = (((1,), (0,)), ((), ()))
NT = (((1,), (1,)), ((), ()))
VARS = 112


def slope(differ):
    return differ * lax.rsqrt(differ * differ + smoothing * smoothing)


def dot(a, b, dims, precision=None):
    return lax.dot_general(a, b, dims, precision=precision, preferred_element_type=F32)


def split(value):
    high = value.astype(BF16)
    return high, (value - high.astype(F32)).astype(BF16)


def ring():
    spot = lax.axis_index("shard")
    return spot, lax.rem(spot + 1, 4), lax.rem(spot + 3, 4), lax.rem(spot + 2, 4)


def signal(barrier, axis, to):
    pl.semaphore_signal(barrier, inc=1, device_id={axis: to}, device_id_type=MESH_ID)


def member_lines(me):
    core = lax.rem(me, 2)
    y = lax.rem(lax.div(me, 2), 4)
    x = lax.rem(lax.div(me, 8), 4)
    z = lax.div(me, 32)
    x_line = [me + 8 * (lax.rem(x + step, 4) - x) for step in (1, 2, 3)]
    y_line = [me + 2 * (lax.rem(y + step, 4) - y) for step in (1, 2, 3)]
    return x_line, y_line, [me + 32 * (1 - 2 * z)], [me + 1 - 2 * core]


def step_kernel(
    members,
    mesh_in,
    stencil_in,
    weight_in,
    prev_in,
    observed_in,
    area_in,
    var_in,
    hidden_in,
    hidden_bias_in,
    output_in,
    output_bias_in,
    out_ref,
    gathered,
    stencil,
    weight,
    prev,
    observed,
    area,
    var,
    output_bias,
    hidden,
    hidden_bias,
    output,
    inverse_ref,
    stack,
    column_sums,
    average_row,
    target,
    coefficient,
    blend,
    blend_t,
    product,
    slope_act,
    grad_side,
    joined,
    forecast_out_a,
    forecast_out_b,
    forecast_in_a,
    forecast_in_b,
    state_b,
    sums_a,
    sums_b,
    cot_out_a,
    cot_out_b,
    cot_in_a,
    cot_in_b,
    result_ref,
    part_out,
    part_hop,
    part_in,
    local_sem,
    known,
    gather_send,
    gather_recv,
    cast_send,
    cast_recv,
    back_send,
    back_recv,
    part_send,
    part_recv,
):
    me = lax.axis_index("member")
    spot, right, left, across = ring()
    lines = member_lines(me)
    barrier = pltpu.get_barrier_semaphore()
    for neighbour in (left, right):
        signal(barrier, "shard", neighbour)
    for line in lines:
        for peer in line:
            signal(barrier, "member", peer)
    loads = [
        pltpu.make_async_copy(source, place, local_sem.at[number])
        for number, (source, place) in enumerate(
            (
                (stencil_in, stencil),
                (weight_in, weight),
                (prev_in, prev),
                (observed_in, observed),
                (area_in, area),
                (var_in, var),
                (output_bias_in, output_bias),
                (mesh_in, gathered.at[pl.ds(2 * spot, 2)]),
                (hidden_in, hidden),
                (hidden_bias_in, hidden_bias),
                (output_in, output.at[pl.ds(0, VARS)]),
            )
        )
    ]
    pl.semaphore_wait(barrier, 10)
    for peer in lines[0]:
        signal(known.at[0], "member", peer)

    def copy(number, source, slot, to):
        return pltpu.make_async_remote_copy(
            src_ref=source,
            dst_ref=gathered.at[slot],
            send_sem=gather_send.at[number],
            recv_sem=gather_recv.at[number],
            device_id={"shard": to},
            device_id_type=MESH_ID,
        )

    own = [
        copy(0, mesh_in.at[0], 2 * spot, right),
        copy(1, mesh_in.at[1], 2 * spot + 1, left),
        copy(2, mesh_in.at[1], 2 * spot + 1, right),
        copy(3, mesh_in.at[0], 2 * spot, left),
    ]
    for each in own:
        each.start()
    for load in loads:
        load.start()
    for load in loads[:7]:
        load.wait()

    row_ids = lax.broadcasted_iota(jnp.int32, (128, 768), 0)
    cells_t = jnp.zeros((128, 768), F32)
    for k in range(3):
        cells_t = cells_t + jnp.where(stencil[k] == row_ids, weight[k], 0.0)
    natural = lax.broadcasted_iota(jnp.int32, (768, 768), 1)
    place = lax.broadcasted_iota(jnp.int32, (768, 768), 0)
    slot = jnp.where(
        place < 512,
        lax.shift_right_logical(place, 3),
        lax.shift_right_logical(place - 512, 2),
    )
    scorer = 2 * (slot & 31) + lax.shift_right_logical(slot, 5)
    cell_of = scorer * 12 + jnp.where(place < 512, place & 7, 8 + (place & 3))
    order = jnp.where(natural == cell_of, 1.0, 0.0).astype(BF16)
    cells_high = cells_t.astype(BF16)
    ordered = dot(order, cells_high, NT).astype(BF16)
    blend[:, :128] = ordered
    blend[:, 128:] = ordered
    blend_t[...] = dot(cells_high, order, NT).astype(BF16)

    slots = lax.broadcasted_iota(jnp.int32, (16, 768), 0)
    slots = jnp.where(slots < 12, slots, slots - 4)
    chosen = jnp.where(
        lax.broadcasted_iota(jnp.int32, (16, 768), 1) == slots + 12 * me, 1.0, 0.0
    ).astype(F32)
    target[...] = jnp.zeros((16, 128), F32)
    for slot in range(16):
        cell = slot if slot < 12 else slot - 4
        target[slot : slot + 1, :VARS] = observed[cell] - output_bias[...]
    target[:, :VARS] = target[:, :VARS] - dot(chosen, prev[...], NT, lax.Precision.HIGHEST)
    lanes = lax.broadcasted_iota(jnp.int32, (16, 12), 1)
    cell_ids = lax.broadcasted_iota(jnp.int32, (16, 12), 0)
    cell_ids = jnp.where(cell_ids < 12, cell_ids, cell_ids - 4)
    area_column = jnp.sum(
        jnp.where(lanes == cell_ids, area[...], 0.0), axis=1, keepdims=True
    )
    coefficient[...] = jnp.zeros((16, 128), F32)
    coefficient[:, :VARS] = area_column * var[...]

    pl.semaphore_wait(known.at[0], 3)
    for peer in lines[1]:
        signal(known.at[1], "member", peer)
    own[0].wait_recv()
    relay_right = copy(4, gathered.at[2 * left], 2 * left, right)
    relay_right.start()
    own[1].wait_recv()
    relay_left = copy(5, gathered.at[2 * right + 1], 2 * right + 1, left)
    relay_left.start()
    pl.semaphore_wait(known.at[1], 3)
    for peer in lines[2]:
        signal(known.at[2], "member", peer)
    output[VARS:] = jnp.zeros((128 - VARS, 1024), BF16)
    for load in loads[7:]:
        load.wait()
    for each in own[2:] + [relay_right, relay_left]:
        each.wait_recv()

    rows_low = gathered[...].reshape(128, 1024)
    rows = rows_low.astype(F32)
    average = jnp.mean(rows, axis=1, keepdims=True)
    row_high, row_low = split(rows - average)
    cross = dot(row_low, row_high, NT)
    gram = (dot(row_high, row_high, NT) + cross + cross.T) * (1.0 / 1024)
    through_all = dot(
        jnp.concatenate([rows_low, jnp.ones((16, 1024), BF16)], axis=0), hidden[...], NN
    )
    column_sums[...] = through_all[128:129]
    diagonal = lax.broadcasted_iota(jnp.int32, (128, 128), 0) == lax.broadcasted_iota(
        jnp.int32, (128, 128), 1
    )
    average_row[...] = jnp.sum(jnp.where(diagonal, average, 0.0), axis=0, keepdims=True)
    through = through_all[:128] - average * through_all[128:129]
    through_high, through_low = split(through)
    stack[:128, :1024] = through_high
    stack[128:, :1024] = through_low
    gram_high, gram_low = split(gram)
    stack[:128, 1024:] = gram_high
    stack[128:, 1024:] = gram_low

    core = lax.rem(me, 2)
    chip = lax.div(me, 2)
    my_slot = core * 32 + chip
    row_y = lax.rem(chip, 4)
    row_x = lax.rem(lax.div(chip, 4), 4)
    row_z = lax.div(chip, 16)
    xs = [4 * lax.rem(row_x + step, 4) for step in range(4)]
    ys = [lax.rem(row_y + step, 4) for step in range(4)]
    zs = [16 * row_z, 16 * (1 - row_z)]
    moves = [
        (z + min(x, 4 - x) + min(y, 4 - y), z, x, y)
        for z in range(2)
        for x in range(4)
        for y in range(4)
        if z + x + y
    ]
    moves.sort(key=lambda move: -move[0])
    chips = [zs[z] + xs[x] + ys[y] for _, z, x, y in moves]

    def exchange(source, source_slot, place, place_slot, to, send, recv):
        pltpu.make_async_remote_copy(
            src_ref=source.at[source_slot],
            dst_ref=place.at[place_slot],
            send_sem=send,
            recv_sem=recv,
            device_id={"member": to},
            device_id_type=MESH_ID,
        ).start()

    def send_forecast(source, place, number, sides):
        def start(other, side):
            exchange(
                source,
                side * 32 + other,
                place,
                me,
                2 * other + side,
                cast_send.at[number],
                cast_recv.at[number],
            )

        for other in chips:
            for side in sides:
                start(other, side)
        if len(sides) == 2:
            start(chip, 1 - core)
        else:

            @pl.when(core != sides[0])
            def _():
                start(chip, sides[0])

    def updates(span):
        raw = dot(blend[span], stack[...], NN)
        variance = jnp.sum(
            raw[:, 1024:] * blend[span, :128].astype(F32), axis=1, keepdims=True
        )
        inverse = lax.rsqrt(variance + epsilon)
        inverse_ref[span] = jnp.broadcast_to(inverse, (256, 128))
        value = raw[:, :1024] * inverse
        product[span] = value
        act = value + hidden_bias[...]
        active = act * (0.5 * jnp.tanh(0.5 * act) + 0.5)
        return dot(active.astype(BF16), output[...], NT)

    pl.semaphore_wait(known.at[2], 1)

    for side in range(2):
        update = updates(pl.ds(side * 256, 256))
        forecast_out_a[pl.ds(side * 32, 32)] = update.reshape(32, 8, 128)
        send_forecast(forecast_out_a, forecast_in_a, 0, (side,))

    update = updates(pl.ds(512, 256))
    for piece in range(64):
        forecast_out_b[piece] = update[piece * 4 : piece * 4 + 4]
    send_forecast(forecast_out_b, forecast_in_b, 1, (0, 1))

    forecast_in_a[me] = forecast_out_a[my_slot]
    forecast_in_b[me] = forecast_out_b[my_slot]

    @pl.loop(0, 6)
    def _(part):
        span = pl.ds(pl.multiple_of(part * 128, 128), 128)
        act = product[span] + hidden_bias[...]
        gate = 0.5 * jnp.tanh(0.5 * act) + 0.5
        slope_act[span] = gate * (1.0 + act * (1.0 - gate)) * inverse_ref[span][:, :1]

    others = pl.ds(0, members - 1)

    def settle(ref, sem):
        pltpu.make_async_copy(ref.at[others], ref.at[others], sem).wait()

    settle(forecast_in_a, cast_recv.at[0])

    @pl.loop(0, 8)
    def _(block):
        base = block * 8
        values = [forecast_in_a[base + i] for i in range(8)]
        totals = [jnp.zeros((8, 128), F32) for _ in range(8)]
        for i in range(8):
            for j in range(i + 1, 8):
                push = slope(values[i] - values[j])
                totals[i] = totals[i] + push
                totals[j] = totals[j] - push
        for i in range(8):
            sums_a[base + i] = totals[i]

    def pair_blocks(first, seconds):
        values = [forecast_in_a[first + i] for i in range(8)]
        totals = [sums_a[first + i] for i in range(8)]
        for second in seconds:
            for j in range(8):
                other = forecast_in_a[second + j]
                total = sums_a[second + j]
                for i in range(8):
                    push = slope(values[i] - other)
                    totals[i] = totals[i] + push
                    total = total - push
                sums_a[second + j] = total
        for i in range(8):
            sums_a[first + i] = totals[i]

    @pl.loop(0, 12)
    def _(step):
        block = lax.rem(step, 8)
        apart = block + 1 + 2 * lax.div(step, 8)
        pair_blocks(block * 8, (lax.rem(apart, 8) * 8, lax.rem(apart + 1, 8) * 8))

    @pl.loop(4, 8)
    def _(block):
        pair_blocks(block * 8, (lax.rem(block + 3, 8) * 8,))

    pair_factor = (1.0 - (1.0 - fairness) / members) / (members - 1)

    @pl.loop(0, 8)
    def _(block):
        for i in range(8):
            m = block * 8 + i
            cot_out_a[m] = (
                coefficient[:8]
                * (slope(forecast_in_a[m] - target[:8]) - pair_factor * sums_a[m])
            ).astype(BF16)

    def send_back(source, place, number):
        def start(to):
            exchange(source, to, place, my_slot, to, back_send.at[number], back_recv.at[number])

        for other in chips:
            for side in range(2):
                start(2 * other + side)
        start(2 * chip + 1 - core)

    send_back(cot_out_a, cot_in_a, 0)
    cot_in_a[my_slot] = cot_out_a[me]

    settle(forecast_in_b, cast_recv.at[1])
    for m in range(32):
        state_b[m] = jnp.concatenate([forecast_in_b[m], forecast_in_b[m + 32]], axis=0)

    def half_turn(value):
        return pltpu.roll(value, 4, 0)

    @pl.loop(0, 4)
    def _(block):
        base = block * 8
        values = [state_b[base + i] for i in range(8)]
        turned = [half_turn(value) for value in values]
        totals = [slope(values[i] - turned[i]) for i in range(8)]
        crossed = [jnp.zeros((8, 128), F32) for _ in range(8)]
        for i in range(8):
            for j in range(i + 1, 8):
                push = slope(values[i] - values[j])
                totals[i] = totals[i] + push
                totals[j] = totals[j] - push
                push = slope(values[i] - turned[j])
                totals[i] = totals[i] + push
                crossed[j] = crossed[j] - push
        for i in range(8):
            sums_b[base + i] = totals[i] + half_turn(crossed[i])

    @pl.loop(0, 6)
    def _(step):
        first = lax.rem(step, 4) * 8
        second = lax.rem(lax.rem(step, 4) + lax.div(step, 4) + 1, 4) * 8
        values = [state_b[first + i] for i in range(8)]
        totals = [sums_b[first + i] for i in range(8)]
        for j in range(8):
            other = state_b[second + j]
            turned = half_turn(other)
            total = sums_b[second + j]
            crossed = jnp.zeros((8, 128), F32)
            for i in range(8):
                push = slope(values[i] - other)
                totals[i] = totals[i] + push
                total = total - push
                push = slope(values[i] - turned)
                totals[i] = totals[i] + push
                crossed = crossed - push
            sums_b[second + j] = total + half_turn(crossed)
        for i in range(8):
            sums_b[first + i] = totals[i]

    @pl.loop(0, 8)
    def _(block):
        for i in range(4):
            m = block * 4 + i
            cot = coefficient[8:] * (
                slope(state_b[m] - target[8:]) - pair_factor * sums_b[m]
            )
            cot_out_b[m] = cot[:4].astype(BF16)
            cot_out_b[m + 32] = cot[4:].astype(BF16)

    send_back(cot_out_b, cot_in_b, 1)
    cot_in_b[my_slot] = cot_out_b[me]

    def backward(cot, span):
        grad = dot(cot, output[...], NN) * slope_act[span]
        grad_side[span, :1024] = grad.astype(BF16)
        along = jnp.sum(grad * product[span], axis=1, keepdims=True) * (1.0 / 1024)
        grad_side[span, 1024:] = (
            blend[span, :128].astype(F32) * (inverse_ref[span] * along)
        ).astype(BF16)

    settle(cot_in_a, back_recv.at[0])

    @pl.loop(0, 4)
    def _(part):
        cot = cot_in_a[pl.ds(part * 16, 16)].astype(F32).reshape(128, 128).astype(BF16)
        backward(cot, pl.ds(pl.multiple_of(part * 128, 128), 128))

    joined[...] = dot(blend_t[:, :512], grad_side[:512], NN)
    settle(cot_in_b, back_recv.at[1])

    @pl.loop(0, 2)
    def _(part):
        cot = jnp.concatenate(
            [cot_in_b[part * 32 + piece].astype(F32) for piece in range(32)], axis=0
        ).astype(BF16)
        backward(cot, pl.ds(pl.multiple_of(512 + part * 128, 128), 128))

    total = joined[...] + dot(blend_t[:, 512:], grad_side[512:], NN)
    outer = total[:, :1024].astype(BF16)
    inner = total[:, 1024:].astype(BF16)
    centre = jnp.sum(
        outer.astype(F32) * column_sums[...], axis=1, keepdims=True
    ) * (1.0 / 1024) - jnp.sum(inner.astype(F32) * average_row[...], axis=1, keepdims=True)

    def part_copy(half, number, source, to):
        return pltpu.make_async_remote_copy(
            src_ref=source,
            dst_ref=part_in.at[half, number],
            send_sem=part_send.at[half, number],
            recv_sem=part_recv.at[half, number],
            device_id={"shard": to},
            device_id_type=MESH_ID,
        )

    halves = []
    for half in range(2):
        wide = slice(half * 512, half * 512 + 512)
        result = dot(outer, hidden[wide], NT)
        result = result - dot(inner, gathered[:, :, wide].reshape(128, 512), NN) - centre
        result_ref[half] = result.reshape(8, 16, 512)
        part_out[half] = result.astype(BF16).reshape(8, 16, 512)
        hops = [
            part_copy(half, 0, part_out.at[half, 2 * across], right),
            part_copy(half, 1, part_out.at[half, 2 * across + 1], left),
            part_copy(half, 2, part_out.at[half, 2 * right + 1], right),
            part_copy(half, 3, part_out.at[half, 2 * left], left),
            part_copy(half, 4, part_hop.at[half, 0], right),
            part_copy(half, 5, part_hop.at[half, 1], left),
        ]
        for hop in hops[:2]:
            hop.start()
        halves.append(hops)
    for hops in halves:
        for hop in hops[2:4]:
            hop.start()
    for half, hops in enumerate(halves):
        hops[0].wait_recv()
        part_hop[half, 0] = (
            part_in[half, 0].astype(F32) + result_ref[half, 2 * right]
        ).astype(BF16)
        hops[4].start()
        hops[1].wait_recv()
        part_hop[half, 1] = (
            part_in[half, 1].astype(F32) + result_ref[half, 2 * left + 1]
        ).astype(BF16)
        hops[5].start()
    for half, hops in enumerate(halves):
        wide = slice(half * 512, half * 512 + 512)
        for hop in hops[2:]:
            hop.wait_recv()
        out_ref[:16, wide] = (
            result_ref[half, 2 * spot]
            + part_in[half, 4].astype(F32)
            + part_in[half, 3].astype(F32)
        )
        out_ref[16:, wide] = (
            result_ref[half, 2 * spot + 1]
            + part_in[half, 2].astype(F32)
            + part_in[half, 5].astype(F32)
        )

    for each in own + [relay_right, relay_left] + halves[0] + halves[1]:
        each.wait_send()
    settle(forecast_out_a, cast_send.at[0])
    settle(forecast_out_b, cast_send.at[1])
    settle(cot_out_a, back_send.at[0])
    settle(cot_out_b, back_send.at[1])


def local(
    processor_latent,
    stencil_index,
    interp_weight,
    prev_state,
    observed,
    cell_area,
    var_weight,
    hidden_weight,
    hidden_bias,
    output_weight,
    output_bias,
):
    members = lax.axis_size("member")
    vmem = pltpu.VMEM
    dma = pltpu.SemaphoreType.DMA

    def body(*refs):
        step_kernel(members, *refs)

    out = pl.pallas_call(
        body,
        name="decoder_step",
        out_shape=jax.ShapeDtypeStruct((32, 1024), F32),
        in_specs=[pl.BlockSpec(memory_space=pl.ANY)] * 11,
        out_specs=pl.BlockSpec(memory_space=pltpu.VMEM),
        scratch_shapes=[
            vmem((8, 16, 1024), BF16),
            vmem((3, 1, 768), jnp.int32),
            vmem((3, 1, 768), F32),
            vmem((112, 768), F32),
            vmem((12, 1, 112), F32),
            vmem((1, 12), F32),
            vmem((1, 112), F32),
            vmem((1, 112), F32),
            vmem((1024, 1024), BF16),
            vmem((1, 1024), F32),
            vmem((128, 1024), BF16),
            vmem((768, 128), F32),
            vmem((256, 1152), BF16),
            vmem((1, 1024), F32),
            vmem((1, 128), F32),
            vmem((16, 128), F32),
            vmem((16, 128), F32),
            vmem((768, 256), BF16),
            vmem((128, 768), BF16),
            vmem((768, 1024), F32),
            vmem((768, 1024), F32),
            vmem((768, 1152), BF16),
            vmem((128, 1152), F32),
            vmem((64, 8, 128), F32),
            vmem((64, 4, 128), F32),
            vmem((64, 8, 128), F32),
            vmem((64, 4, 128), F32),
            vmem((32, 8, 128), F32),
            vmem((64, 8, 128), F32),
            vmem((32, 8, 128), F32),
            vmem((64, 8, 128), BF16),
            vmem((64, 4, 128), BF16),
            vmem((64, 8, 128), BF16),
            vmem((64, 4, 128), BF16),
            vmem((2, 8, 16, 512), F32),
            vmem((2, 8, 16, 512), BF16),
            vmem((2, 2, 16, 512), BF16),
            vmem((2, 6, 16, 512), BF16),
            dma((11,)),
            pltpu.SemaphoreType.REGULAR((3,)),
            dma((6,)),
            dma((6,)),
            dma((2,)),
            dma((2,)),
            dma((2,)),
            dma((2,)),
            dma((2, 6)),
            dma((2, 6)),
        ],
        compiler_params=pltpu.CompilerParams(
            collective_id=0, has_side_effects=True, vmem_limit_bytes=40 << 20
        ),
    )(
        *(
            pltpu.with_memory_space_constraint(each, pltpu.MemorySpace.HBM)
            for each in (
                processor_latent.reshape(2, 16, 1024),
                jnp.transpose(stencil_index, (1, 0, 2)),
                jnp.transpose(interp_weight, (1, 0, 2)),
                prev_state[0],
                jnp.transpose(observed, (2, 0, 1)),
                cell_area,
                var_weight.reshape(1, -1),
                hidden_weight,
                hidden_bias.reshape(1, -1),
                output_weight.T,
                output_bias.reshape(1, -1),
            )
        )
    )
    return out[None]


def solution(mesh):
    in_specs = (
        P("member", "shard", None),
        P("shard", None, None),
        P("shard", None, None),
        P("shard", None, None),
        P("shard", None, "member"),
        P("shard", "member"),
        P(),
        P(),
        P(),
        P(),
        P(),
    )
    out_specs = P("member", "shard", None)
    return jax.shard_map(local, mesh=mesh, in_specs=in_specs, out_specs=out_specs, check_vma=False)
```

```python
import jax
import jax.numpy as jnp
from jax import lax
from jax.experimental import pallas as pl
from jax.experimental.pallas import tpu as pltpu
from jax.sharding import PartitionSpec as P

smoothing = 0.05
fairness = 0.95
epsilon = 1e-05

MESH_ID = pl.DeviceIdType.MESH
F32 = jnp.float32
BF16 = jnp.bfloat16
NN = (((1,), (0,)), ((), ()))
NT = (((1,), (1,)), ((), ()))
VARS = 112


def slope(differ):
    return differ * lax.rsqrt(differ * differ + smoothing * smoothing)


def dot(a, b, dims, precision=None):
    return lax.dot_general(a, b, dims, precision=precision, preferred_element_type=F32)


def split(value):
    high = value.astype(BF16)
    return high, (value - high.astype(F32)).astype(BF16)


def ring():
    spot = lax.axis_index("shard")
    return spot, lax.rem(spot + 1, 4), lax.rem(spot + 3, 4), lax.rem(spot + 2, 4)


def signal(barrier, axis, to):
    pl.semaphore_signal(barrier, inc=1, device_id={axis: to}, device_id_type=MESH_ID)


def member_lines(me):
    core = lax.rem(me, 2)
    y = lax.rem(lax.div(me, 2), 4)
    x = lax.rem(lax.div(me, 8), 4)
    z = lax.div(me, 32)
    x_line = [me + 8 * (lax.rem(x + step, 4) - x) for step in (1, 2, 3)]
    y_line = [me + 2 * (lax.rem(y + step, 4) - y) for step in (1, 2, 3)]
    return x_line, y_line, [me + 32 * (1 - 2 * z)], [me + 1 - 2 * core]


def step_kernel(
    members,
    mesh_in,
    stencil_in,
    weight_in,
    prev_in,
    observed_in,
    area_in,
    var_in,
    hidden_in,
    hidden_bias_in,
    output_in,
    output_bias_in,
    out_ref,
    gathered,
    stencil,
    weight,
    prev,
    observed,
    area,
    var,
    output_bias,
    hidden,
    hidden_bias,
    output,
    inverse_ref,
    stack,
    column_sums,
    average_row,
    target,
    coefficient,
    blend,
    blend_t,
    product,
    slope_act,
    grad_side,
    joined,
    forecast_out_a,
    forecast_out_b,
    forecast_in_a,
    forecast_in_b,
    state_b,
    sums_a,
    sums_b,
    cot_out_a,
    cot_out_b,
    cot_in_a,
    cot_in_b,
    result_ref,
    part_out,
    part_hop,
    part_in,
    local_sem,
    known,
    gather_send,
    gather_recv,
    cast_send,
    cast_recv,
    back_send,
    back_recv,
    part_send,
    part_recv,
):
    me = lax.axis_index("member")
    spot, right, left, across = ring()
    lines = member_lines(me)
    barrier = pltpu.get_barrier_semaphore()
    for neighbour in (left, right):
        signal(barrier, "shard", neighbour)
    for line in lines:
        for peer in line:
            signal(barrier, "member", peer)
    loads = [
        pltpu.make_async_copy(source, place, local_sem.at[number])
        for number, (source, place) in enumerate(
            (
                (stencil_in, stencil),
                (weight_in, weight),
                (prev_in, prev),
                (observed_in, observed),
                (area_in, area),
                (var_in, var),
                (output_bias_in, output_bias),
                (mesh_in, gathered.at[pl.ds(4 * spot, 4)]),
                (hidden_in, hidden),
                (hidden_bias_in, hidden_bias),
                (output_in, output.at[pl.ds(0, VARS)]),
            )
        )
    ]
    pl.semaphore_wait(barrier, 10)
    for peer in lines[0]:
        signal(known.at[0], "member", peer)

    def copy(number, source, slot, to):
        return pltpu.make_async_remote_copy(
            src_ref=source,
            dst_ref=gathered.at[slot],
            send_sem=gather_send.at[number],
            recv_sem=gather_recv.at[number],
            device_id={"shard": to},
            device_id_type=MESH_ID,
        )

    to_right = [copy(i, mesh_in.at[i], 4 * spot + i, right) for i in range(4)]
    to_left = [copy(7 - i, mesh_in.at[i], 4 * spot + i, left) for i in (3, 2, 1, 0)]
    for pair in zip(to_right, to_left):
        for each in pair:
            each.start()
    for load in loads:
        load.start()
    for load in loads[:7]:
        load.wait()

    row_ids = lax.broadcasted_iota(jnp.int32, (128, 768), 0)
    cells_t = jnp.zeros((128, 768), F32)
    for k in range(3):
        cells_t = cells_t + jnp.where(stencil[k] == row_ids, weight[k], 0.0)
    natural = lax.broadcasted_iota(jnp.int32, (768, 768), 1)
    place = lax.broadcasted_iota(jnp.int32, (768, 768), 0)
    slot = jnp.where(
        place < 512,
        lax.shift_right_logical(place, 3),
        lax.shift_right_logical(place - 512, 2),
    )
    scorer = 2 * (slot & 31) + lax.shift_right_logical(slot, 5)
    cell_of = scorer * 12 + jnp.where(place < 512, place & 7, 8 + (place & 3))
    order = jnp.where(natural == cell_of, 1.0, 0.0).astype(BF16)
    cells_high = cells_t.astype(BF16)
    ordered = dot(order, cells_high, NT).astype(BF16)
    blend[:, :128] = ordered
    blend[:, 128:] = ordered
    blend_t[...] = dot(cells_high, order, NT).astype(BF16)

    slots = lax.broadcasted_iota(jnp.int32, (16, 768), 0)
    slots = jnp.where(slots < 12, slots, slots - 4)
    chosen = jnp.where(
        lax.broadcasted_iota(jnp.int32, (16, 768), 1) == slots + 12 * me, 1.0, 0.0
    ).astype(F32)
    target[...] = jnp.zeros((16, 128), F32)
    for slot in range(16):
        cell = slot if slot < 12 else slot - 4
        target[slot : slot + 1, :VARS] = observed[cell] - output_bias[...]
    target[:, :VARS] = target[:, :VARS] - dot(chosen, prev[...], NT, lax.Precision.HIGHEST)
    lanes = lax.broadcasted_iota(jnp.int32, (16, 12), 1)
    cell_ids = lax.broadcasted_iota(jnp.int32, (16, 12), 0)
    cell_ids = jnp.where(cell_ids < 12, cell_ids, cell_ids - 4)
    area_column = jnp.sum(
        jnp.where(lanes == cell_ids, area[...], 0.0), axis=1, keepdims=True
    )
    coefficient[...] = jnp.zeros((16, 128), F32)
    coefficient[:, :VARS] = area_column * var[...]

    pl.semaphore_wait(known.at[0], 3)
    for peer in lines[1]:
        signal(known.at[1], "member", peer)
    relays = []
    for i in range(2):
        to_right[i].wait_recv()
        relays.append(copy(8 + i, gathered.at[4 * left + i], 4 * left + i, right))
        relays[-1].start()
        to_left[i].wait_recv()
        relays.append(copy(10 + i, gathered.at[4 * right + 3 - i], 4 * right + 3 - i, left))
        relays[-1].start()
    pl.semaphore_wait(known.at[1], 3)
    for peer in lines[2]:
        signal(known.at[2], "member", peer)
    output[VARS:] = jnp.zeros((128 - VARS, 1024), BF16)
    for load in loads[7:]:
        load.wait()
    for each in to_right[2:] + to_left[2:] + relays:
        each.wait_recv()

    rows_low = gathered[...].reshape(128, 1024)
    rows = rows_low.astype(F32)
    average = jnp.mean(rows, axis=1, keepdims=True)
    row_high, row_low = split(rows - average)
    cross = dot(row_low, row_high, NT)
    gram = (dot(row_high, row_high, NT) + cross + cross.T) * (1.0 / 1024)
    through_all = dot(
        jnp.concatenate([rows_low, jnp.ones((16, 1024), BF16)], axis=0), hidden[...], NN
    )
    column_sums[...] = through_all[128:129]
    diagonal = lax.broadcasted_iota(jnp.int32, (128, 128), 0) == lax.broadcasted_iota(
        jnp.int32, (128, 128), 1
    )
    average_row[...] = jnp.sum(jnp.where(diagonal, average, 0.0), axis=0, keepdims=True)
    through = through_all[:128] - average * through_all[128:129]
    through_high, through_low = split(through)
    stack[:128, :1024] = through_high
    stack[128:, :1024] = through_low
    gram_high, gram_low = split(gram)
    stack[:128, 1024:] = gram_high
    stack[128:, 1024:] = gram_low

    core = lax.rem(me, 2)
    chip = lax.div(me, 2)
    my_slot = core * 32 + chip
    row_y = lax.rem(chip, 4)
    row_x = lax.rem(lax.div(chip, 4), 4)
    row_z = lax.div(chip, 16)
    xs = [4 * lax.rem(row_x + step, 4) for step in range(4)]
    ys = [lax.rem(row_y + step, 4) for step in range(4)]
    zs = [16 * row_z, 16 * (1 - row_z)]
    moves = [
        (z + min(x, 4 - x) + min(y, 4 - y), z, x, y)
        for z in range(2)
        for x in range(4)
        for y in range(4)
        if z + x + y
    ]
    moves.sort(key=lambda move: -move[0])
    chips = [zs[z] + xs[x] + ys[y] for _, z, x, y in moves]

    def exchange(source, source_slot, place, place_slot, to, send, recv):
        pltpu.make_async_remote_copy(
            src_ref=source.at[source_slot],
            dst_ref=place.at[place_slot],
            send_sem=send,
            recv_sem=recv,
            device_id={"member": to},
            device_id_type=MESH_ID,
        ).start()

    def send_forecast(source, place, number, sides):
        def start(other, side):
            exchange(
                source,
                side * 32 + other,
                place,
                me,
                2 * other + side,
                cast_send.at[number],
                cast_recv.at[number],
            )

        for other in chips:
            for side in sides:
                start(other, side)
        if len(sides) == 2:
            start(chip, 1 - core)
        else:

            @pl.when(core != sides[0])
            def _():
                start(chip, sides[0])

    def updates(span):
        raw = dot(blend[span], stack[...], NN)
        variance = jnp.sum(
            raw[:, 1024:] * blend[span, :128].astype(F32), axis=1, keepdims=True
        )
        inverse = lax.rsqrt(variance + epsilon)
        inverse_ref[span] = jnp.broadcast_to(inverse, (256, 128))
        value = raw[:, :1024] * inverse
        product[span] = value
        act = value + hidden_bias[...]
        active = act * (0.5 * jnp.tanh(0.5 * act) + 0.5)
        return dot(active.astype(BF16), output[...], NT)

    pl.semaphore_wait(known.at[2], 1)

    for side in range(2):
        update = updates(pl.ds(side * 256, 256))
        forecast_out_a[pl.ds(side * 32, 32)] = update.reshape(32, 8, 128)
        send_forecast(forecast_out_a, forecast_in_a, 0, (side,))

    update = updates(pl.ds(512, 256))
    for piece in range(64):
        forecast_out_b[piece] = update[piece * 4 : piece * 4 + 4]
    send_forecast(forecast_out_b, forecast_in_b, 1, (0, 1))

    forecast_in_a[me] = forecast_out_a[my_slot]
    forecast_in_b[me] = forecast_out_b[my_slot]

    @pl.loop(0, 6)
    def _(part):
        span = pl.ds(pl.multiple_of(part * 128, 128), 128)
        act = product[span] + hidden_bias[...]
        gate = 0.5 * jnp.tanh(0.5 * act) + 0.5
        slope_act[span] = gate * (1.0 + act * (1.0 - gate)) * inverse_ref[span][:, :1]

    others = pl.ds(0, members - 1)

    def settle(ref, sem):
        pltpu.make_async_copy(ref.at[others], ref.at[others], sem).wait()

    settle(forecast_in_a, cast_recv.at[0])

    @pl.loop(0, 8)
    def _(block):
        base = block * 8
        values = [forecast_in_a[base + i] for i in range(8)]
        totals = [jnp.zeros((8, 128), F32) for _ in range(8)]
        for i in range(8):
            for j in range(i + 1, 8):
                push = slope(values[i] - values[j])
                totals[i] = totals[i] + push
                totals[j] = totals[j] - push
        for i in range(8):
            sums_a[base + i] = totals[i]

    def pair_blocks(first, seconds):
        values = [forecast_in_a[first + i] for i in range(8)]
        totals = [sums_a[first + i] for i in range(8)]
        for second in seconds:
            for j in range(8):
                other = forecast_in_a[second + j]
                total = sums_a[second + j]
                for i in range(8):
                    push = slope(values[i] - other)
                    totals[i] = totals[i] + push
                    total = total - push
                sums_a[second + j] = total
        for i in range(8):
            sums_a[first + i] = totals[i]

    @pl.loop(0, 12)
    def _(step):
        block = lax.rem(step, 8)
        apart = block + 1 + 2 * lax.div(step, 8)
        pair_blocks(block * 8, (lax.rem(apart, 8) * 8, lax.rem(apart + 1, 8) * 8))

    @pl.loop(4, 8)
    def _(block):
        pair_blocks(block * 8, (lax.rem(block + 3, 8) * 8,))

    pair_factor = (1.0 - (1.0 - fairness) / members) / (members - 1)

    @pl.loop(0, 8)
    def _(block):
        for i in range(8):
            m = block * 8 + i
            cot_out_a[m] = (
                coefficient[:8]
                * (slope(forecast_in_a[m] - target[:8]) - pair_factor * sums_a[m])
            ).astype(BF16)

    def send_back(source, place, number):
        def start(to):
            exchange(source, to, place, my_slot, to, back_send.at[number], back_recv.at[number])

        for other in chips:
            for side in range(2):
                start(2 * other + side)
        start(2 * chip + 1 - core)

    send_back(cot_out_a, cot_in_a, 0)
    cot_in_a[my_slot] = cot_out_a[me]

    settle(forecast_in_b, cast_recv.at[1])
    for m in range(32):
        state_b[m] = jnp.concatenate([forecast_in_b[m], forecast_in_b[m + 32]], axis=0)

    def half_turn(value):
        return pltpu.roll(value, 4, 0)

    @pl.loop(0, 4)
    def _(block):
        base = block * 8
        values = [state_b[base + i] for i in range(8)]
        turned = [half_turn(value) for value in values]
        totals = [slope(values[i] - turned[i]) for i in range(8)]
        crossed = [jnp.zeros((8, 128), F32) for _ in range(8)]
        for i in range(8):
            for j in range(i + 1, 8):
                push = slope(values[i] - values[j])
                totals[i] = totals[i] + push
                totals[j] = totals[j] - push
                push = slope(values[i] - turned[j])
                totals[i] = totals[i] + push
                crossed[j] = crossed[j] - push
        for i in range(8):
            sums_b[base + i] = totals[i] + half_turn(crossed[i])

    @pl.loop(0, 6)
    def _(step):
        first = lax.rem(step, 4) * 8
        second = lax.rem(lax.rem(step, 4) + lax.div(step, 4) + 1, 4) * 8
        values = [state_b[first + i] for i in range(8)]
        totals = [sums_b[first + i] for i in range(8)]
        for j in range(8):
            other = state_b[second + j]
            turned = half_turn(other)
            total = sums_b[second + j]
            crossed = jnp.zeros((8, 128), F32)
            for i in range(8):
                push = slope(values[i] - other)
                totals[i] = totals[i] + push
                total = total - push
                push = slope(values[i] - turned)
                totals[i] = totals[i] + push
                crossed = crossed - push
            sums_b[second + j] = total + half_turn(crossed)
        for i in range(8):
            sums_b[first + i] = totals[i]

    @pl.loop(0, 8)
    def _(block):
        for i in range(4):
            m = block * 4 + i
            cot = coefficient[8:] * (
                slope(state_b[m] - target[8:]) - pair_factor * sums_b[m]
            )
            cot_out_b[m] = cot[:4].astype(BF16)
            cot_out_b[m + 32] = cot[4:].astype(BF16)

    send_back(cot_out_b, cot_in_b, 1)
    cot_in_b[my_slot] = cot_out_b[me]

    def backward(cot, span):
        grad = dot(cot, output[...], NN) * slope_act[span]
        grad_side[span, :1024] = grad.astype(BF16)
        along = jnp.sum(grad * product[span], axis=1, keepdims=True) * (1.0 / 1024)
        grad_side[span, 1024:] = (
            blend[span, :128].astype(F32) * (inverse_ref[span] * along)
        ).astype(BF16)

    settle(cot_in_a, back_recv.at[0])

    @pl.loop(0, 4)
    def _(part):
        cot = cot_in_a[pl.ds(part * 16, 16)].astype(F32).reshape(128, 128).astype(BF16)
        backward(cot, pl.ds(pl.multiple_of(part * 128, 128), 128))

    joined[...] = dot(blend_t[:, :512], grad_side[:512], NN)
    settle(cot_in_b, back_recv.at[1])

    @pl.loop(0, 2)
    def _(part):
        cot = jnp.concatenate(
            [cot_in_b[part * 32 + piece].astype(F32) for piece in range(32)], axis=0
        ).astype(BF16)
        backward(cot, pl.ds(pl.multiple_of(512 + part * 128, 128), 128))

    total = joined[...] + dot(blend_t[:, 512:], grad_side[512:], NN)
    outer = total[:, :1024].astype(BF16)
    inner = total[:, 1024:].astype(BF16)
    centre = jnp.sum(
        outer.astype(F32) * column_sums[...], axis=1, keepdims=True
    ) * (1.0 / 1024) - jnp.sum(inner.astype(F32) * average_row[...], axis=1, keepdims=True)

    def part_copy(half, number, source, to):
        return pltpu.make_async_remote_copy(
            src_ref=source,
            dst_ref=part_in.at[half, number],
            send_sem=part_send.at[half, number],
            recv_sem=part_recv.at[half, number],
            device_id={"shard": to},
            device_id_type=MESH_ID,
        )

    halves = []
    for half in range(2):
        wide = slice(half * 512, half * 512 + 512)
        result = dot(outer, hidden[wide], NT)
        result = result - dot(inner, gathered[:, :, wide].reshape(128, 512), NN) - centre
        result_ref[half] = result.reshape(8, 16, 512)
        part_out[half] = result.astype(BF16).reshape(8, 16, 512)
        hops = [
            part_copy(half, 0, part_out.at[half, 2 * across], right),
            part_copy(half, 1, part_out.at[half, 2 * across + 1], left),
            part_copy(half, 2, part_out.at[half, 2 * right + 1], right),
            part_copy(half, 3, part_out.at[half, 2 * left], left),
            part_copy(half, 4, part_hop.at[half, 0], right),
            part_copy(half, 5, part_hop.at[half, 1], left),
        ]
        for hop in hops[:2]:
            hop.start()
        halves.append(hops)
    for hops in halves:
        for hop in hops[2:4]:
            hop.start()
    for half, hops in enumerate(halves):
        hops[0].wait_recv()
        part_hop[half, 0] = (
            part_in[half, 0].astype(F32) + result_ref[half, 2 * right]
        ).astype(BF16)
        hops[4].start()
        hops[1].wait_recv()
        part_hop[half, 1] = (
            part_in[half, 1].astype(F32) + result_ref[half, 2 * left + 1]
        ).astype(BF16)
        hops[5].start()
    for half, hops in enumerate(halves):
        wide = slice(half * 512, half * 512 + 512)
        for hop in hops[2:]:
            hop.wait_recv()
        out_ref[:16, wide] = (
            result_ref[half, 2 * spot]
            + part_in[half, 4].astype(F32)
            + part_in[half, 3].astype(F32)
        )
        out_ref[16:, wide] = (
            result_ref[half, 2 * spot + 1]
            + part_in[half, 2].astype(F32)
            + part_in[half, 5].astype(F32)
        )

    for each in to_right + to_left + relays + halves[0] + halves[1]:
        each.wait_send()
    settle(forecast_out_a, cast_send.at[0])
    settle(forecast_out_b, cast_send.at[1])
    settle(cot_out_a, back_send.at[0])
    settle(cot_out_b, back_send.at[1])


def local(
    processor_latent,
    stencil_index,
    interp_weight,
    prev_state,
    observed,
    cell_area,
    var_weight,
    hidden_weight,
    hidden_bias,
    output_weight,
    output_bias,
):
    members = lax.axis_size("member")
    vmem = pltpu.VMEM
    dma = pltpu.SemaphoreType.DMA

    def body(*refs):
        step_kernel(members, *refs)

    out = pl.pallas_call(
        body,
        name="decoder_step",
        out_shape=jax.ShapeDtypeStruct((32, 1024), F32),
        in_specs=[pl.BlockSpec(memory_space=pl.ANY)] * 11,
        out_specs=pl.BlockSpec(memory_space=pltpu.VMEM),
        scratch_shapes=[
            vmem((16, 8, 1024), BF16),
            vmem((3, 1, 768), jnp.int32),
            vmem((3, 1, 768), F32),
            vmem((112, 768), F32),
            vmem((12, 1, 112), F32),
            vmem((1, 12), F32),
            vmem((1, 112), F32),
            vmem((1, 112), F32),
            vmem((1024, 1024), BF16),
            vmem((1, 1024), F32),
            vmem((128, 1024), BF16),
            vmem((768, 128), F32),
            vmem((256, 1152), BF16),
            vmem((1, 1024), F32),
            vmem((1, 128), F32),
            vmem((16, 128), F32),
            vmem((16, 128), F32),
            vmem((768, 256), BF16),
            vmem((128, 768), BF16),
            vmem((768, 1024), F32),
            vmem((768, 1024), F32),
            vmem((768, 1152), BF16),
            vmem((128, 1152), F32),
            vmem((64, 8, 128), F32),
            vmem((64, 4, 128), F32),
            vmem((64, 8, 128), F32),
            vmem((64, 4, 128), F32),
            vmem((32, 8, 128), F32),
            vmem((64, 8, 128), F32),
            vmem((32, 8, 128), F32),
            vmem((64, 8, 128), BF16),
            vmem((64, 4, 128), BF16),
            vmem((64, 8, 128), BF16),
            vmem((64, 4, 128), BF16),
            vmem((2, 8, 16, 512), F32),
            vmem((2, 8, 16, 512), BF16),
            vmem((2, 2, 16, 512), BF16),
            vmem((2, 6, 16, 512), BF16),
            dma((11,)),
            pltpu.SemaphoreType.REGULAR((3,)),
            dma((12,)),
            dma((12,)),
            dma((2,)),
            dma((2,)),
            dma((2,)),
            dma((2,)),
            dma((2, 6)),
            dma((2, 6)),
        ],
        compiler_params=pltpu.CompilerParams(
            collective_id=0, has_side_effects=True, vmem_limit_bytes=40 << 20
        ),
    )(
        *(
            pltpu.with_memory_space_constraint(each, pltpu.MemorySpace.HBM)
            for each in (
                processor_latent.reshape(4, 8, 1024),
                jnp.transpose(stencil_index, (1, 0, 2)),
                jnp.transpose(interp_weight, (1, 0, 2)),
                prev_state[0],
                jnp.transpose(observed, (2, 0, 1)),
                cell_area,
                var_weight.reshape(1, -1),
                hidden_weight,
                hidden_bias.reshape(1, -1),
                output_weight.T,
                output_bias.reshape(1, -1),
            )
        )
    )
    return out[None]


def solution(mesh):
    in_specs = (
        P("member", "shard", None),
        P("shard", None, None),
        P("shard", None, None),
        P("shard", None, None),
        P("shard", None, "member"),
        P("shard", "member"),
        P(),
        P(),
        P(),
        P(),
        P(),
    )
    out_specs = P("member", "shard", None)
    return jax.shard_map(local, mesh=mesh, in_specs=in_specs, out_specs=out_specs, check_vma=False)
```
